128 devices in a mesh: cfg: 2 (over y_hi), seq: 8 (over z, y_lo), tp: 8 (over x, core).
Axes of the slice: x: 4, y: 4 (y_hi: 2, y_lo: 2; y = y_hi * 2 + y_lo), z: 4, core: 2. Of those that a mesh axis runs over, the one named last changes fastest.
Arguments:
- hidden_in: bfloat16 [2, 4, 1536, 3072], P('cfg', None, 'seq', 'tp'), as said below
- w_qkv: bfloat16 [3072, 3, 3072], P(None, None, 'tp')
- w_mlp: bfloat16 [3072, 6144], P(None, 'tp'), may hold values from -0.109375 to 0.109375
- w_attn_out: bfloat16 [3072, 3072], P('tp'), may hold values from -0.109375 to 0.109375
- w_mlp_out: bfloat16 [6144, 3072], P('tp'), may hold values from -0.0625 to 0.0625
- mod_table: float32 [28, 3, 3072], replicated, may hold values from -6 to 6
- qk_gain: float32 [2, 128], replicated, as said below
- timestep: int32 [4], replicated, may hold values from 0 to 27
- text_len: int32 [2, 4], P('cfg'), may hold values from 128 to 512
- pos_ids: int32 [4, 3, 1536], P(None, None, 'seq'), may hold values from 0 to 158, as said below
Outputs:
- guided: bfloat16 [4, 1536, 3072], P('cfg', 'seq', 'tp')
- state_norm: float32 [2, 4], P('cfg')
- max_logit: float32 [2, 4], P('cfg')
The draws below stay inside these ranges and needn't reach their ends.
Inputs may be any that keep to these rules, and one draw needn't show every extreme that they name: `hidden_in`: the entries have scales that differ between tokens and between features. `qk_gain`: positive gains. `pos_ids`: text tokens have ids 0 on all axes; image token i of a request (token 512 + i) has ids 0, i // 32 + a and i % 32 + b, with offsets a and b of the request in 0 to 127; one request has both offsets 4 * 32 - 1.
All inputs are finite; a program needn't handle non-finite values.
Results may differ from the reference program's by a relative error of at most 0.0025.
Values may be sent and summed in bfloat16 or wider, within the bound.
No kernel may reach another device: no remote copies, remote signals or barrier semaphores. Data moves between devices by JAX's collectives and lax.ppermute only.
A program may use at most 128 MiB of HBM per device.

```python
import math
import jax
import jax.numpy as jnp
from jax import lax

D = 3072
HEADS = 24
HD = 128
FF = 6144
TXT = 512
GRID = 32
STEPS = 28
REQ = 4
SEQ_LEN = 1536
INNER = 3072


def draw_hidden_in(key, part):
    key_base, key_rows, key_cols = jax.random.split(key, 3)
    shape = (2, REQ, SEQ_LEN, D)
    position = jnp.arange(SEQ_LEN, dtype=jnp.int32)
    rising = jnp.power(3.0, position.astype(jnp.float32) / SEQ_LEN)[None, None, :, None]
    col_scale = jnp.exp(jax.random.uniform(key_cols, (1, 1, 1, D), jnp.float32, 0.0, math.log(3.0)))
    base_draw = jax.random.normal(key_base, shape, jnp.float32)
    row_scale = jnp.exp(jax.random.uniform(key_rows, (2, REQ, SEQ_LEN, 1), jnp.float32, 0.0, math.log(3.0)))
    values = base_draw * row_scale * rising * col_scale
    return values.astype(jnp.bfloat16)


def draw_w_qkv(key, part):
    key_base = jax.random.fold_in(key, 0)
    base_draw = jax.random.normal(key_base, (D, 3, INNER), jnp.float32) / math.sqrt(D)
    return base_draw.astype(jnp.bfloat16)


def draw_qk_gain(key, part):
    return jnp.exp(jax.random.uniform(key, (2, HD), jnp.float32, math.log(1.2), math.log(2.4)))


def draw_pos_ids(key, part):
    key_offsets, key_chosen = jax.random.split(key, 2)
    offsets = jax.random.randint(key_offsets, (REQ, 2), 0, 4 * GRID)
    chosen = jax.random.randint(key_chosen, (), 0, REQ)
    is_chosen = jnp.arange(REQ, dtype=jnp.int32)[:, None] == chosen
    offsets = jnp.where(is_chosen, 4 * GRID - 1, offsets).astype(jnp.int32)
    image_index = jnp.arange(SEQ_LEN, dtype=jnp.int32) - TXT
    is_image = image_index >= 0
    safe_index = jnp.maximum(image_index, 0)
    row_ids = jnp.where(is_image[None, :], safe_index[None, :] // GRID + offsets[:, 0:1], 0)
    col_ids = jnp.where(is_image[None, :], safe_index[None, :] % GRID + offsets[:, 1:2], 0)
    zero_ids = jnp.zeros((REQ, SEQ_LEN), jnp.int32)
    return jnp.stack([zero_ids, row_ids, col_ids], axis=1).astype(jnp.int32)


def set_ends(array, own_key, least, high):
    extent = array.shape
    index_at = [jax.random.randint(jax.random.fold_in(own_key, axis), (), 0, extent[axis]) for axis in range(len(extent))]
    array = array.at[tuple(index_at)].set(least)
    longest = extent.index(max(extent))
    index_at[longest] = (index_at[longest] + 1) % extent[longest]
    return array.at[tuple(index_at)].set(high)


def levels(own_key, extent, shards, smallest, largest):
    def one(dim, shards_of):
        draws = jax.random.uniform(jax.random.fold_in(jax.random.fold_in(own_key, 6), dim), (shards_of,), jnp.float32, smallest / len(shards), largest / len(shards))
        return jnp.repeat(jnp.exp(draws), extent[dim] // shards_of).reshape((-1,) + (1,) * (len(extent) - dim - 1))

    loudness = one(*shards[0])
    for cut in shards[1:]:
        loudness = loudness * one(*cut)
    return loudness


def noise(stream_key, extent, deviation, most, cuts=(), held_as=jnp.bfloat16):
    result = deviation * jax.random.normal(stream_key, extent, jnp.float32)
    if cuts:
        result = result * levels(stream_key, extent, cuts, -0.22, 0.18)
    return jnp.clip(result, -most, most).astype(held_as)


def setup_inputs(seed: int = 0) -> dict:
    key_list = jax.random.split(jax.random.key(seed), 11)
    hidden_in = draw_hidden_in(jax.random.fold_in(key_list[10], 71), 0)
    w_qkv = draw_w_qkv(jax.random.fold_in(key_list[10], 71), 0)
    w_mlp = noise(key_list[2], (D, FF), D ** -0.5, 0.109375, ((1, 8),))
    w_attn_out = noise(key_list[3], (INNER, D), INNER ** -0.5, 0.109375, ((0, 8),))
    w_mlp_out = noise(key_list[4], (FF, D), (INNER + FF) ** -0.5, 0.0625, ((0, 8),))
    mod_table = noise(key_list[5], (STEPS, 3, D), 1.0, 6.0, (), jnp.float32)
    qk_gain = draw_qk_gain(jax.random.fold_in(key_list[10], 71), 0)
    timestep = set_ends(jax.random.randint(key_list[7], (REQ,), 0, STEPS), jax.random.fold_in(key_list[7], 1), 0, STEPS - 1).astype(jnp.int32)
    text_len = set_ends(jax.random.randint(key_list[8], (2, REQ), TXT // 4, TXT + 1), jax.random.fold_in(key_list[8], 1), TXT // 4, TXT).astype(jnp.int32)
    pos_ids = draw_pos_ids(jax.random.fold_in(key_list[10], 71), 0)
    return dict(hidden_in=hidden_in, w_qkv=w_qkv, w_mlp=w_mlp, w_attn_out=w_attn_out, w_mlp_out=w_mlp_out, mod_table=mod_table, qk_gain=qk_gain, timestep=timestep, text_len=text_len, pos_ids=pos_ids)


norm_eps = 1e-06
rope_theta = 10000.0
guidance_scale = 4.0
rescale_share = 0.7
masked_value = -1e+30

def lookup_rows(mod_table, timestep):
    step_count = mod_table.shape[0]
    onehot = timestep[:, None] == jnp.arange(step_count, dtype=jnp.int32)[None, :]
    return lax.optimization_barrier(jnp.sum(jnp.where(onehot[:, :, None, None], mod_table[None], jnp.float32(0.0)), axis=1))

def rope_tables(pos_ids, head_size):
    pair_index = jnp.arange(head_size, dtype=jnp.int32) // 2
    first_end = head_size // 16
    second = first_end + (head_size - head_size // 8) // 4
    axis_of = jnp.where(pair_index < first_end, 0, jnp.where(pair_index < second, 1, 2))
    offset = pair_index - jnp.where(axis_of == 0, 0, jnp.where(axis_of == 1, first_end, second))
    pair_span = jnp.where(axis_of == 0, head_size // 8, (head_size - head_size // 8) // 2)
    frequency = jnp.power(jnp.float32(rope_theta), -2.0 * offset.astype(jnp.float32) / pair_span.astype(jnp.float32))
    angles = jnp.zeros((pos_ids.shape[0], pos_ids.shape[2], head_size), jnp.float32)
    for axis_id in range(3):
        column = jnp.where(axis_of == axis_id, frequency, jnp.float32(0.0))
        angles = angles + pos_ids[:, axis_id, :, None].astype(jnp.float32) * column[None, None, :]
    row_ids = jnp.arange(head_size, dtype=jnp.int32)[:, None]
    col_ids = jnp.arange(head_size, dtype=jnp.int32)[None, :]
    swapper = jnp.where((col_ids % 2 == 0) & (row_ids == col_ids + 1), -1.0, jnp.where((col_ids % 2 == 1) & (row_ids == col_ids - 1), 1.0, 0.0)).astype(jnp.float32)
    return (jnp.cos(angles), jnp.sin(angles), swapper)

def head_norm(values, gain_row):
    return values * lax.rsqrt(lax.optimization_barrier(jnp.mean(values * values, axis=-1, keepdims=True)) + norm_eps) * gain_row

def rotate(values, cosine, sine_table, swapper):
    turned = jnp.einsum('rshd,de->rshe', values, swapper, precision=lax.Precision.HIGHEST)
    return values * cosine[:, :, None, :] + turned * sine_table[:, :, None, :]

def modulate(tokens, modulation):
    values = tokens.astype(jnp.float32)
    center = values - lax.optimization_barrier(jnp.mean(values, axis=-1, keepdims=True))
    normed = center * lax.rsqrt(lax.optimization_barrier(jnp.mean(center * center, axis=-1, keepdims=True)) + norm_eps)
    return ((1.0 + modulation[:, 1, None, :]) * normed + modulation[:, 0, None, :]).astype(jnp.bfloat16)

def reference(hidden_in, w_qkv, w_mlp, w_attn_out, w_mlp_out, mod_table, qk_gain, timestep, text_len, pos_ids):
    modulation = lookup_rows(mod_table, timestep)
    cosine, sine_table, swapper = rope_tables(pos_ids, HD)
    positions = jnp.arange(SEQ_LEN, dtype=jnp.int32)
    score_scale = HD ** (-0.5)
    new_states = []
    peak_list = []
    for copy_id in range(2):
        tokens = hidden_in[copy_id]
        modded = modulate(tokens, modulation)
        flat_rows = modded.reshape(REQ * SEQ_LEN, D)
        projected = jnp.dot(flat_rows, w_qkv.reshape(D, 3 * INNER), preferred_element_type=jnp.float32)
        projected = projected.reshape(REQ, SEQ_LEN, 3, HEADS, HD)
        queries = rotate(head_norm(projected[:, :, 0], qk_gain[0]), cosine, sine_table, swapper).astype(jnp.bfloat16)
        key_all = rotate(head_norm(projected[:, :, 1], qk_gain[1]), cosine, sine_table, swapper).astype(jnp.bfloat16)
        value_all = projected[:, :, 2].astype(jnp.bfloat16)
        usable = (positions[None, :] >= TXT) | (positions[None, :] < text_len[copy_id][:, None])

        def attend_head(operands):
            query_head, key_head, value_head = operands
            scores = jnp.einsum('rqd,rkd->rqk', query_head.astype(jnp.float32), key_head.astype(jnp.float32)) * score_scale
            scores = jnp.where(usable[:, None, :], scores, masked_value)
            row_peak = lax.optimization_barrier(jnp.max(scores, axis=-1))
            weights = jnp.where(usable[:, None, :], jnp.exp(scores - row_peak[..., None]), 0.0)
            weight_sum = lax.optimization_barrier(jnp.sum(weights, axis=-1))
            rounded = lax.optimization_barrier(weights.astype(jnp.bfloat16))
            mixture = jnp.einsum('rqk,rkd->rqd', rounded.astype(jnp.float32), value_head.astype(jnp.float32))
            return (mixture / weight_sum[..., None], lax.optimization_barrier(jnp.max(row_peak, axis=-1)))
        mixture, head_peaks = lax.map(attend_head, (jnp.transpose(queries, (2, 0, 1, 3)), jnp.transpose(key_all, (2, 0, 1, 3)), jnp.transpose(value_all, (2, 0, 1, 3))))
        attended = jnp.transpose(mixture, (1, 2, 0, 3)).reshape(REQ * SEQ_LEN, INNER).astype(jnp.bfloat16)
        hidden_units = jax.nn.gelu(jnp.dot(flat_rows, w_mlp, preferred_element_type=jnp.float32), approximate=True).astype(jnp.bfloat16)
        branch = jnp.dot(attended, w_attn_out, preferred_element_type=jnp.float32) + jnp.dot(hidden_units, w_mlp_out, preferred_element_type=jnp.float32)
        new_state = tokens.astype(jnp.float32) + modulation[:, 2, None, :] * branch.reshape(REQ, SEQ_LEN, D)
        new_states.append(new_state)
        peak_list.append(lax.optimization_barrier(jnp.max(head_peaks, axis=0)))
    entries = float(SEQ_LEN * D)
    conditional = new_states[0]
    unconditional = new_states[1]
    raw = unconditional + guidance_scale * (conditional - unconditional)
    norms = [jnp.sqrt(lax.optimization_barrier(jnp.sum(one * one, axis=(1, 2))) / entries + norm_eps) for one in new_states]
    raw_norm = jnp.sqrt(lax.optimization_barrier(jnp.sum(raw * raw, axis=(1, 2))) / entries + norm_eps)
    factor = rescale_share * norms[0] / raw_norm + (1.0 - rescale_share)
    guided = (raw * factor[:, None, None]).astype(jnp.bfloat16)
    return (guided, jnp.stack(norms, axis=0), jnp.stack(peak_list, axis=0))
```

```python
import functools

import jax
import jax.numpy as jnp
from jax import lax
from jax.experimental import pallas as pl
from jax.experimental.pallas import tpu as pltpu
from jax.sharding import PartitionSpec as P

D = 3072
TXT = 512
SEQ_LEN = 1536
GRID = 32
HD = 128

norm_eps = 1e-06
rope_theta = 10000.0
guidance_scale = 4.0
rescale_share = 0.7
masked_value = -1e30


f32 = jnp.float32
bf16 = jnp.bfloat16

SWAP = [(i, i ^ 1) for i in range(8)]
CFG_SWAP = [(0, 1), (1, 0)]


def shift4(k):
    return [(i, ((i // 2 + k) % 4) * 2 + i % 2) for i in range(8)]


def xor4(p):
    return [(i, ((i // 2) ^ p) * 2 + i % 2) for i in range(8)]


def home_perm(j):
    pairs = []
    for c in range(2):
        for s in range(8):
            r = s // 2
            slot = c * 2 + r % 2
            pairs.append((c * 8 + s, (r // 2) * 8 + (slot ^ j) * 2 + s % 2))
    return pairs


def pick(array, index):
    return lax.dynamic_index_in_dim(array, index, 0, False)


def ln_kernel(order, *refs):
    blocks, scale_ref, shift_ref, out_ref = refs[:8], refs[8], refs[9], refs[10]
    width = blocks[0].shape[1]
    total = None
    for ref in blocks:
        part = jnp.sum(ref[...].astype(f32), axis=-1, keepdims=True)
        total = part if total is None else total + part
    mean = total * (1.0 / D)
    square = None
    for ref in blocks:
        center = ref[...].astype(f32) - mean
        part = jnp.sum(center * center, axis=-1, keepdims=True)
        square = part if square is None else square + part
    inverse = lax.rsqrt(square * (1.0 / D) + norm_eps)
    for n, ref in enumerate(blocks):
        cols = pl.ds(pl.multiple_of(order[n] * width, 128), width)
        normed = (ref[...].astype(f32) - mean) * inverse
        out_ref[:, cols] = ((1.0 + scale_ref[:, cols]) * normed + shift_ref[:, cols]).astype(bf16)


def layer_norm(order, blocks, scale, shift):
    rows, width = blocks[0].shape
    tile = 128
    return pl.pallas_call(
        ln_kernel,
        grid_spec=pltpu.PrefetchScalarGridSpec(
            num_scalar_prefetch=1,
            grid=(rows // tile,),
            in_specs=[pl.BlockSpec((tile, width), lambda i, o: (i, 0))] * 8
            + [pl.BlockSpec((1, D), lambda i, o: (0, 0))] * 2,
            out_specs=pl.BlockSpec((tile, D), lambda i, o: (i, 0)),
        ),
        out_shape=jax.ShapeDtypeStruct((rows, D), bf16),
        cost_estimate=pl.CostEstimate(flops=rows * D * 12, transcendentals=0, bytes_accessed=rows * D * 4),
        name="layer_norm",
    )(order, *blocks, scale, shift)


def rotary(values, gain_row, cosine, sine):
    heads = []
    lane = lax.broadcasted_iota(jnp.int32, cosine.shape, 1)
    even = lane % 2 == 0
    for h in range(values.shape[1] // HD):
        u = values[:, h * HD : (h + 1) * HD]
        u = u * lax.rsqrt(jnp.mean(u * u, axis=-1, keepdims=True) + norm_eps) * gain_row
        turned = jnp.where(even, -pltpu.roll(u, HD - 1, 1), pltpu.roll(u, 1, 1))
        heads.append(u * cosine + turned * sine)
    return jnp.concatenate(heads, axis=1)


def kv_kernel(m_ref, wk_ref, wv_ref, gain_ref, cos_ref, sin_ref, k_ref, v_ref):
    m = m_ref[...]
    keys = jnp.dot(m, wk_ref[...], preferred_element_type=f32)
    k_ref[...] = rotary(keys, gain_ref[...], cos_ref[...], sin_ref[...]).astype(bf16)
    v_ref[...] = jnp.dot(m, wv_ref[...], preferred_element_type=f32).astype(bf16)


def q_kernel(m_ref, wq_ref, gain_ref, cos_ref, sin_ref, q_ref):
    queries = jnp.dot(m_ref[...], wq_ref[...], preferred_element_type=f32)
    q_ref[...] = rotary(queries, gain_ref[...], cos_ref[...], sin_ref[...]).astype(bf16)


def project(kernel, name, modded, weights, gain, cosine, sine):
    rows = modded.shape[0]
    inner = weights[0].shape[1]
    tile = 192
    n = len(weights)
    row = lambda i: (i, 0)
    fixed = lambda i: (0, 0)
    return pl.pallas_call(
        kernel,
        grid=(rows // tile,),
        in_specs=[pl.BlockSpec((tile, D), row)]
        + [pl.BlockSpec((D, inner), fixed)] * n
        + [pl.BlockSpec((1, HD), fixed), pl.BlockSpec((tile, HD), row), pl.BlockSpec((tile, HD), row)],
        out_specs=[pl.BlockSpec((tile, inner), row)] * n,
        out_shape=[jax.ShapeDtypeStruct((rows, inner), bf16)] * n,
        cost_estimate=pl.CostEstimate(
            flops=2 * rows * D * inner * n, transcendentals=0, bytes_accessed=(rows * D + n * inner * D) * 2
        ),
        name=name,
    )(modded, *weights, gain, cosine, sine)


def attention_kernel(q_ref, ka_ref, kb_ref, va_ref, vb_ref, ba_ref, bb_ref, o_ref, peak_ref):
    contract = (((1,), (1,)), ((), ()))
    scale = HD ** (-0.5)
    q = q_ref[...]
    sa = lax.dot_general(q, ka_ref[...], contract, preferred_element_type=f32) * scale + ba_ref[...]
    sb = lax.dot_general(q, kb_ref[...], contract, preferred_element_type=f32) * scale + bb_ref[...]
    peak = jnp.maximum(jnp.max(sa, axis=-1, keepdims=True), jnp.max(sb, axis=-1, keepdims=True))
    wa = jnp.exp(sa - peak)
    wb = jnp.exp(sb - peak)
    total = jnp.sum(wa, axis=-1, keepdims=True) + jnp.sum(wb, axis=-1, keepdims=True)
    mix = jnp.dot(wa.astype(bf16), va_ref[...], preferred_element_type=f32) + jnp.dot(
        wb.astype(bf16), vb_ref[...], preferred_element_type=f32
    )
    o_ref[...] = (mix / total).astype(bf16)
    top = jnp.max(peak)

    @pl.when((pl.program_id(0) == 0) & (pl.program_id(1) == 0))
    def _():
        peak_ref[...] = jnp.full(peak_ref.shape, top, f32)

    peak_ref[...] = jnp.maximum(peak_ref[...], top)


def attention(q, ka, kb, va, vb, ba, bb):
    rows, inner = q.shape
    keys = ka.shape[0]
    tile = 256
    head = lambda h, i: (0, h)
    fixed = lambda h, i: (0, 0)
    return pl.pallas_call(
        attention_kernel,
        grid=(inner // HD, rows // tile),
        in_specs=[pl.BlockSpec((tile, HD), lambda h, i: (i, h))]
        + [pl.BlockSpec((keys, HD), head)] * 4
        + [pl.BlockSpec((1, keys), fixed)] * 2,
        out_specs=[pl.BlockSpec((tile, HD), lambda h, i: (i, h)), pl.BlockSpec((8, 128), fixed)],
        out_shape=[jax.ShapeDtypeStruct((rows, inner), bf16), jax.ShapeDtypeStruct((8, 128), f32)],
        cost_estimate=pl.CostEstimate(
            flops=8 * rows * keys * inner, transcendentals=2 * rows * keys * 3, bytes_accessed=rows * inner * 12
        ),
        name="attention",
    )(q, ka, kb, va, vb, ba, bb)


def out_kernel(order, a_ref, h_ref, wa_ref, wh_ref, o_ref):
    total = jnp.dot(a_ref[...], wa_ref[...], preferred_element_type=f32)
    total += jnp.dot(h_ref[...], wh_ref[...], preferred_element_type=f32)
    o_ref[...] = total[None].astype(o_ref.dtype)


def out_project(order, attended, units, w_attn_out, w_mlp_out, dtype, width):
    rows, inner = attended.shape
    hidden = units.shape[1]
    count = order.shape[0]
    fixed = lambda n, o: (0, 0)
    return pl.pallas_call(
        out_kernel,
        grid_spec=pltpu.PrefetchScalarGridSpec(
            num_scalar_prefetch=1,
            grid=(count,),
            in_specs=[
                pl.BlockSpec((rows, inner), fixed),
                pl.BlockSpec((rows, hidden), fixed),
                pl.BlockSpec((inner, width), lambda n, o: (0, o[n])),
                pl.BlockSpec((hidden, width), lambda n, o: (0, o[n])),
            ],
            out_specs=pl.BlockSpec((1, rows, width), lambda n, o: (n, 0, 0)),
        ),
        out_shape=jax.ShapeDtypeStruct((count, rows, width), dtype),
        cost_estimate=pl.CostEstimate(
            flops=2 * rows * (inner + hidden) * width * count,
            transcendentals=0,
            bytes_accessed=(rows + width * count) * (inner + hidden) * 2,
        ),
        name="out_project",
    )(order, attended, units, w_attn_out, w_mlp_out)


def rotary_tables(pos_ids, z, y):
    local_len = pos_ids.shape[2]
    image = (2 * z + y) * local_len + jnp.arange(local_len, dtype=jnp.int32) - TXT
    is_image = (image >= 0)[None, :]
    row_offset = jnp.max(jnp.where(is_image, pos_ids[:, 1] - (image // GRID)[None, :], -1), axis=1)
    col_offset = jnp.max(jnp.where(is_image, pos_ids[:, 2] - (image % GRID)[None, :], -1), axis=1)
    mine = jnp.stack([row_offset, col_offset], axis=0)
    above = lax.ppermute(mine, "seq", shift4(3))
    offsets = jnp.where(z == 0, above, mine)
    offsets = lax.dynamic_index_in_dim(offsets, z, 1, False)
    blocks = jnp.arange(4, dtype=jnp.int32)
    shard = 2 * ((z - blocks) % 4) + y
    position = (shard[:, None] * local_len + jnp.arange(local_len, dtype=jnp.int32)[None, :]).reshape(-1)
    index = position - TXT
    pair_index = jnp.arange(HD, dtype=jnp.int32) // 2
    first_end = HD // 16
    second = first_end + (HD - HD // 8) // 4
    axis_of = jnp.where(pair_index < first_end, 0, jnp.where(pair_index < second, 1, 2))
    start = jnp.where(axis_of == 0, 0, jnp.where(axis_of == 1, first_end, second))
    span = jnp.where(axis_of == 0, HD // 8, (HD - HD // 8) // 2)
    frequency = jnp.power(f32(rope_theta), -2.0 * (pair_index - start).astype(f32) / span.astype(f32))
    row_id = jnp.where(index >= 0, index // GRID + offsets[0], 0).astype(f32)
    col_id = jnp.where(index >= 0, index % GRID + offsets[1], 0).astype(f32)
    angles = row_id[:, None] * jnp.where(axis_of == 1, frequency, 0.0)[None, :]
    angles = angles + col_id[:, None] * jnp.where(axis_of == 2, frequency, 0.0)[None, :]
    return jnp.cos(angles), jnp.sin(angles), position


def reduce_all(vector, sums):
    lane = jnp.arange(vector.shape[1])[None, :]
    join = lambda a, b: jnp.where(lane < sums, a + b, jnp.maximum(a, b))
    vector = join(vector, lax.ppermute(vector, "tp", SWAP))
    for p in (1, 2):
        vector = join(vector, lax.ppermute(vector, "tp", xor4(p)))
    for p in (1, 2):
        vector = join(vector, lax.ppermute(vector, "seq", xor4(p)))
    return join(vector, lax.ppermute(vector, "seq", SWAP))


def local(
    hidden_in, w_qkv, w_mlp, w_attn_out, w_mlp_out, mod_table, qk_gain, timestep, text_len, pos_ids
):
    tokens = hidden_in[0]
    requests, local_len, width = tokens.shape
    inner = w_qkv.shape[2]
    group = lax.axis_index("cfg")
    seq = lax.axis_index("seq")
    z, y = seq // 2, seq % 2
    tp = lax.axis_index("tp")
    x, core = tp // 2, tp % 2

    moved = [pick(tokens, z)] + [
        lax.ppermute(pick(tokens, (z + k) % 4), "seq", shift4(k)) for k in range(1, 4)
    ]
    own = jnp.concatenate(moved, axis=0)
    rows = own.shape[0]

    from_x = [own] + [lax.ppermute(own, "tp", shift4(k)) for k in range(1, 4)]
    from_core = [lax.ppermute(block, "tp", SWAP) for block in from_x]
    steps = jnp.arange(4, dtype=jnp.int32)
    back = 2 * ((x - steps) % 4)
    order = jnp.concatenate([back + core, back + 1 - core]).astype(jnp.int32)

    half = requests // 2
    kept = lax.dynamic_slice_in_dim(tokens, half * group, half, 0)
    other = lax.ppermute(
        lax.dynamic_slice_in_dim(tokens, half * (1 - group), half, 0), "cfg", CFG_SWAP
    )

    modulation = pick(mod_table, pick(timestep, z))
    cosine, sine, position = rotary_tables(pos_ids, z, y)

    modded = layer_norm(order, from_x + from_core, modulation[1:2], modulation[0:1])
    wq, wk, wv = w_qkv[:, 0], w_qkv[:, 1], w_qkv[:, 2]
    keys, values = project(kv_kernel, "project_kv", modded, (wk, wv), qk_gain[1:2], cosine, sine)
    keys_far = lax.ppermute(keys, "seq", SWAP)
    values_far = lax.ppermute(values, "seq", SWAP)
    (queries,) = project(q_kernel, "project_q", modded, (wq,), qk_gain[0:1], cosine, sine)
    units = jax.nn.gelu(
        jnp.dot(modded, w_mlp, preferred_element_type=f32), approximate=True
    ).astype(bf16)

    length = pick(text_len[0], z)
    near_pos = position
    far_pos = position + (1 - 2 * y) * local_len
    bias = lambda pos: jnp.where((pos >= TXT) | (pos < length), 0.0, masked_value).astype(f32)[None, :]
    attended, peak = attention(
        queries, keys, keys_far, values, values_far, bias(near_pos), bias(far_pos)
    )

    ahead = 2 * ((x + steps) % 4)
    far_part = out_project(
        (ahead + 1 - core).astype(jnp.int32), attended, units, w_attn_out, w_mlp_out, bf16, width
    )
    got = lax.ppermute(far_part, "tp", SWAP)
    near_part = out_project(
        (ahead + core).astype(jnp.int32), attended, units, w_attn_out, w_mlp_out, f32, width
    )
    joined = [near_part[k] + got[k].astype(f32) for k in range(4)]
    branch = joined[0]
    for k in range(1, 4):
        branch = branch + lax.ppermute(joined[k].astype(bf16), "tp", shift4(k)).astype(f32)

    gate = lax.dynamic_slice_in_dim(modulation[2], tp * width, width, 0)
    delta = (gate[None, :] * branch).astype(bf16).reshape(4, local_len, width)
    slot = group * 2 + z % 2
    landed = [
        lax.ppermute(pick(delta, (z - (slot ^ j)) % 4), ("cfg", "seq"), home_perm(j)) for j in range(4)
    ]
    landed = jnp.stack(landed, axis=0)
    change = [pick(landed, z ^ s).astype(f32) for s in range(4)]
    cond_in = jnp.where(group == 0, kept, other).astype(f32)
    free_in = jnp.where(group == 0, other, kept).astype(f32)
    conditional = cond_in + jnp.stack(change[:2], axis=0)
    unconditional = free_in + jnp.stack(change[2:], axis=0)
    raw = unconditional + guidance_scale * (conditional - unconditional)

    squares = jnp.stack([jnp.sum(v * v, axis=(1, 2)) for v in (conditional, unconditional, raw)])
    mine = jnp.arange(requests)[None, :] // half == group
    spread = jnp.where(mine, jnp.tile(squares, (1, 2)), 0.0).reshape(-1)
    top = jnp.where(jnp.arange(requests) == z, peak[0, 0], masked_value)
    vector = jnp.zeros((1, 128), f32)
    vector = vector.at[0, :12].set(spread).at[0, 12:16].set(top)
    vector = reduce_all(vector, 12)
    opposite = lax.ppermute(vector, "cfg", CFG_SWAP)

    entries = float(SEQ_LEN * D)
    norm = jnp.sqrt(vector[0, :12].reshape(3, requests) / entries + norm_eps)
    factors = rescale_share * norm[0] / norm[2] + (1.0 - rescale_share)
    factor = lax.dynamic_slice_in_dim(factors, half * group, half, 0)
    guided = (raw * factor[:, None, None]).astype(bf16)
    both = (vector + opposite)[0, :8].reshape(2, requests)
    state_norm = jnp.sqrt(pick(both, group) / entries + norm_eps)
    return (guided, state_norm[None, :], vector[0, 12:16][None, :])


def solution(mesh):
    placed = (
        P("cfg", None, "seq", "tp"),
        P(None, None, "tp"),
        P(None, "tp"),
        P("tp", None),
        P("tp", None),
        P(),
        P(),
        P(),
        P("cfg", None),
        P(None, None, "seq"),
    )
    return jax.shard_map(
        local,
        mesh=mesh,
        in_specs=placed,
        out_specs=(P("cfg", "seq", "tp"), P("cfg", None), P("cfg", None)),
        check_vma=False,
    )
```

```python
import functools

import jax
import jax.numpy as jnp
from jax import lax
from jax.experimental import pallas as pl
from jax.experimental.pallas import tpu as pltpu
from jax.sharding import PartitionSpec as P


D = 3072
TXT = 512
SEQ_LEN = 1536
GRID = 32
HD = 128

norm_eps = 1e-06
rope_theta = 10000.0
guidance_scale = 4.0
rescale_share = 0.7
masked_value = -1e30

CHUNKS = 2


f32 = jnp.float32
bf16 = jnp.bfloat16

SWAP = [(i, i ^ 1) for i in range(8)]
CFG_SWAP = [(0, 1), (1, 0)]


def shift4(k):
    return [(i, ((i // 2 + k) % 4) * 2 + i % 2) for i in range(8)]


def owned_shard(g, z, i):
    return (z + g) % 2 + 2 * (i ^ g)


def home_perm(i):
    return [
        (g * 8 + s, (s // 4) * 8 + owned_shard(g, s // 2, i) * 2 + s % 2)
        for g in range(2)
        for s in range(8)
    ]


def send(value, axes, pairs):
    return lax.ppermute(value, axes, pairs)


def together(*values):
    return lax.optimization_barrier(values)


def pick(array, index):
    return lax.dynamic_index_in_dim(array, index, 0, False)


VMEM = pl.BlockSpec(memory_space=pltpu.VMEM)
SMEM = pl.BlockSpec(memory_space=pltpu.SMEM)


HBM = pl.BlockSpec(memory_space=pltpu.HBM)


def call(kernel, outs, args, flops, specs, out_specs, scratch, grant):
    shapes = [jax.ShapeDtypeStruct(shape, dtype) for shape, dtype in outs]
    return pl.pallas_call(
        kernel,
        in_specs=specs,
        out_specs=out_specs,
        out_shape=shapes,
        scratch_shapes=scratch,
        compiler_params=pltpu.CompilerParams(vmem_limit_bytes=grant << 20),
        cost_estimate=pl.CostEstimate(
            flops=flops, transcendentals=0, bytes_accessed=sum(v.size * v.dtype.itemsize for v in args)
        ),
    )(*args)


def rotary(values, gain_row, cosine, sine, even):
    u = values * lax.rsqrt(jnp.mean(values * values, axis=-1, keepdims=True) + norm_eps) * gain_row
    turned = jnp.where(even, -pltpu.roll(u, HD - 1, 1), pltpu.roll(u, 1, 1))
    return u * cosine + turned * sine


def even_lanes(shape):
    return lax.broadcasted_iota(jnp.int32, shape, 1) % 2 == 0


LN_ROWS = 64
DOT_COLS = 256


def kv_kernel(order, *refs):
    blocks = refs[:8]
    scale_ref, shift_ref, w_ref, gain_ref, cos_ref, sin_ref, m_ref, kv_ref = refs[8:]
    rows, width = blocks[0].shape
    pieces = width // 128

    def norm(i, _):
        r = pl.ds(pl.multiple_of(i * LN_ROWS, LN_ROWS), LN_ROWS)

        def pieces_of(ref):
            return [ref[r, n * 128 : (n + 1) * 128].astype(f32) for n in range(pieces)]

        total = jnp.zeros((LN_ROWS, 128), f32)
        for ref in blocks:
            for v in pieces_of(ref):
                total = total + v
        mean = jnp.sum(total, axis=-1, keepdims=True) * (1.0 / D)
        square = jnp.zeros((LN_ROWS, 128), f32)
        for ref in blocks:
            for v in pieces_of(ref):
                center = v - mean
                square = square + center * center
        inverse = lax.rsqrt(jnp.sum(square, axis=-1, keepdims=True) * (1.0 / D) + norm_eps)
        for b, ref in enumerate(blocks):
            for n, v in enumerate(pieces_of(ref)):
                cols = pl.ds(pl.multiple_of(order[b] * width + n * 128, 128), 128)
                normed = (v - mean) * inverse
                m_ref[r, cols] = (scale_ref[:, cols] * normed + shift_ref[:, cols]).astype(bf16)
        return 0

    lax.fori_loop(0, rows // LN_ROWS, norm, 0)
    even = even_lanes((rows, HD))
    inner = w_ref.shape[1] // 2
    for n in range(w_ref.shape[1] // DOT_COLS):
        both = jnp.dot(
            m_ref[...], w_ref[:, n * DOT_COLS : (n + 1) * DOT_COLS], preferred_element_type=f32
        )
        for h in range(DOT_COLS // HD):
            v = both[:, h * HD : (h + 1) * HD]
            at = n * DOT_COLS + h * HD
            if at < inner:
                v = rotary(v, gain_ref[...], cos_ref[...], sin_ref[...], even)
            kv_ref[:, at : at + HD] = v.astype(bf16)


def keys_values(order, blocks, scale, shift, weight, gain, cosine, sine):
    rows = blocks[0].shape[0]
    args = (order, *blocks, scale, shift, weight, gain, cosine, sine)
    return call(
        kv_kernel,
        [((rows, D), bf16), ((rows, weight.shape[1]), bf16)],
        args,
        2 * rows * D * weight.shape[1],
        [SMEM] + [VMEM] * 14,
        [VMEM, VMEM],
        [],
        8,
    )


def qu_kernel(m_ref, wq_ref, wm_ref, wo_ref, gain_ref, cos_ref, sin_ref, q_ref, part_ref, u_ref):
    rows = m_ref.shape[0]
    even = even_lanes((rows, HD))
    for h in range(q_ref.shape[1] // HD):
        c = slice(h * HD, (h + 1) * HD)
        if h % 2 == 0:
            wide = slice(h * HD, min((h + 2) * HD, q_ref.shape[1]))
            pair = jnp.dot(m_ref[...], wq_ref[:, wide], preferred_element_type=f32)
        q = pair[:, (h % 2) * HD : (h % 2 + 1) * HD]
        q_ref[:, c] = rotary(q, gain_ref[...], cos_ref[...], sin_ref[...], even).astype(bf16)

    for n in range(wm_ref.shape[1] // DOT_COLS):
        c = slice(n * DOT_COLS, (n + 1) * DOT_COLS)
        u = jnp.dot(m_ref[...], wm_ref[:, c], preferred_element_type=f32)
        u_ref[:, c] = jax.nn.gelu(u, approximate=True).astype(bf16)

    def part(n, _):
        c = pl.ds(pl.multiple_of(n * DOT_COLS, DOT_COLS), DOT_COLS)
        part_ref[:, c] = jnp.dot(u_ref[...], wo_ref[:, c], preferred_element_type=f32)
        return 0

    lax.fori_loop(0, D // DOT_COLS, part, 0)


def queries_units(modded, wq, wm, wo, gain, cosine, sine):
    rows = modded.shape[0]
    inner, hidden = wq.shape[1], wm.shape[1]
    args = (modded, wq, wm, wo, gain, cosine, sine)
    return call(
        qu_kernel,
        [((rows, inner), bf16), ((rows, D), f32)],
        args,
        2 * rows * D * (inner + 2 * hidden),
        [VMEM] * 7,
        [VMEM] * 2,
        [pltpu.VMEM((rows, hidden), bf16)],
        8,
    )


Q_ROWS = 192
LOG2E = 1.4426950408889634


def attention_kernel(order, place, q_ref, *refs):
    kvs = refs[:4]
    w_ref, part_ref, o_ref, far_ref, peak_ref = refs[4:]
    rows, inner = o_ref.shape
    width = far_ref.shape[2]
    piece = rows // 4
    z, y, length = place[0], place[1], place[2]
    lane = lax.broadcasted_iota(jnp.int32, (1, rows), 1)
    block = sum((lane >= k * piece).astype(jnp.int32) for k in range(1, 4))
    biases = []
    for n in range(4):
        shard = 2 * ((z - block) & 3) + (y if n < 2 else 1 - y)
        position = shard * (2 * piece) + (n % 2) * piece + lane - block * piece
        usable = (position >= TXT) | (position < length)
        biases.append(jnp.where(usable, 0.0, masked_value).astype(f32))
    contract = (((1,), (1,)), ((), ()))
    scale = HD ** (-0.5)

    def tile(i, top):
        r = pl.ds(pl.multiple_of(i * Q_ROWS, Q_ROWS), Q_ROWS)
        for h in range(inner // HD):
            c = slice(h * HD, (h + 1) * HD)
            cv = slice(inner + h * HD, inner + (h + 1) * HD)
            q = q_ref[r, c]
            logits = [
                lax.dot_general(q, kv[:, c], contract, preferred_element_type=f32) + bias
                for kv, bias in zip(kvs, biases)
            ]
            peak = functools.reduce(jnp.maximum, [jnp.max(s, axis=-1, keepdims=True) for s in logits])
            total, mix = None, None
            for kv, s in zip(kvs, logits):
                w = jnp.exp2((s - peak) * (scale * LOG2E))
                part = jnp.sum(w, axis=-1, keepdims=True)
                prod = jnp.dot(w.astype(bf16), kv[:, cv], preferred_element_type=f32)
                total = part if total is None else total + part
                mix = prod if mix is None else mix + prod
            o_ref[r, c] = (mix / total).astype(bf16)
            top = jnp.maximum(top, jnp.max(peak))
        return top

    top = lax.fori_loop(0, rows // Q_ROWS, tile, f32(masked_value))
    peak_ref[...] = jnp.full(peak_ref.shape, top * scale, f32)
    for n in range(4):
        cols = pl.ds(pl.multiple_of(order[n] * width, 128), width)
        far_ref[n] = (
            part_ref[:, cols] + jnp.dot(o_ref[...], w_ref[:, cols], preferred_element_type=f32)
        ).astype(bf16)


def attention(order, place, q, kvs, w_attn_out, parts):
    rows, inner = q.shape
    args = (order, place, q, *kvs, w_attn_out, parts)
    return call(
        attention_kernel,
        [((rows, inner), bf16), ((4, rows, D // 8), bf16), ((8, 128), f32)],
        args,
        24 * rows * rows * inner,
        [SMEM] * 2 + [VMEM] * 7,
        [VMEM] * 3,
        [],
        8,
    )


def near_kernel(order, a_ref, w_ref, part_ref, got_ref, *out_refs):
    width = got_ref.shape[2]
    for n, o_ref in enumerate(out_refs):
        cols = pl.ds(pl.multiple_of(order[n] * width, 128), width)
        total = part_ref[:, cols] + jnp.dot(a_ref[...], w_ref[:, cols], preferred_element_type=f32)
        o_ref[...] = (total + got_ref[n].astype(f32)).astype(o_ref.dtype)


def near_project(order, attended, w_attn_out, parts, got):
    rows, inner = attended.shape
    return call(
        near_kernel,
        [((rows, D // 8), f32)] + [((rows, D // 8), bf16)] * 3,
        (order, attended, w_attn_out, parts, got),
        rows * inner * D,
        [SMEM] + [VMEM] * 4,
        [VMEM] * 4,
        [],
        8,
    )


def rotary_tables(pos_ids, z, y, w_qkv):
    local_len = pos_ids.shape[2]
    image = (2 * z + y) * local_len + jnp.arange(local_len, dtype=jnp.int32) - TXT
    is_image = (image >= 0)[None, :]
    row_offset = jnp.max(jnp.where(is_image, pos_ids[:, 1] - (image // GRID)[None, :], -1), axis=1)
    col_offset = jnp.max(jnp.where(is_image, pos_ids[:, 2] - (image % GRID)[None, :], -1), axis=1)
    mine = jnp.stack([row_offset, col_offset], axis=0)
    above = send(mine, "seq", shift4(3))
    above, w_qkv = together(above, w_qkv)
    offsets = jnp.where(z == 0, above, mine)
    offsets = lax.dynamic_index_in_dim(offsets, z, 1, False)
    blocks = jnp.arange(4, dtype=jnp.int32)
    shard = 2 * ((z - blocks) % 4) + y
    part = local_len // CHUNKS
    start = jnp.arange(CHUNKS, dtype=jnp.int32)[:, None, None] * part + jnp.arange(part, dtype=jnp.int32)
    position = (shard[None, :, None] * local_len + start).reshape(-1)
    index = position - TXT
    pair_index = jnp.arange(HD, dtype=jnp.int32) // 2
    first_end = HD // 16
    second = first_end + (HD - HD // 8) // 4
    axis_of = jnp.where(pair_index < first_end, 0, jnp.where(pair_index < second, 1, 2))
    start = jnp.where(axis_of == 0, 0, jnp.where(axis_of == 1, first_end, second))
    span = jnp.where(axis_of == 0, HD // 8, (HD - HD // 8) // 2)
    frequency = jnp.power(f32(rope_theta), -2.0 * (pair_index - start).astype(f32) / span.astype(f32))
    row_id = jnp.where(index >= 0, index // GRID + offsets[0], 0).astype(f32)
    col_id = jnp.where(index >= 0, index % GRID + offsets[1], 0).astype(f32)
    angles = row_id[:, None] * jnp.where(axis_of == 1, frequency, 0.0)[None, :]
    angles = angles + col_id[:, None] * jnp.where(axis_of == 2, frequency, 0.0)[None, :]
    return jnp.cos(angles), jnp.sin(angles), w_qkv


def reduce_all(vector, sums):
    lane = lax.broadcasted_iota(jnp.int32, vector.shape, 1)
    every = jnp.broadcast_to(vector[None], (128,) + vector.shape)
    every = lax.all_to_all(every, ("cfg", "seq", "tp"), 0, 0, tiled=True)
    return jnp.where(lane < sums, jnp.sum(every, axis=0), jnp.max(every, axis=0))


def local(
    hidden_in, w_qkv, w_mlp, w_attn_out, w_mlp_out, mod_table, qk_gain, timestep, text_len, pos_ids
):
    tokens = hidden_in[0]
    requests, local_len, width = tokens.shape
    inner = w_qkv.shape[2]
    group = lax.axis_index("cfg")
    seq = lax.axis_index("seq")
    z, y = seq // 2, seq % 2
    tp = lax.axis_index("tp")
    x, core = tp // 2, tp % 2

    part = local_len // CHUNKS
    rows = 4 * part
    steps = jnp.arange(4, dtype=jnp.int32)
    back = 2 * ((x - steps) % 4)
    order = jnp.concatenate([back + core, back + 1 - core]).astype(jnp.int32)
    ahead = 2 * ((x + steps) % 4)
    near_order = (ahead + core).astype(jnp.int32)
    far_order = (ahead + 1 - core).astype(jnp.int32)

    moved = [pick(tokens, z)] + [
        send(pick(tokens, (z + k) % 4), "seq", shift4(k)) for k in range(1, 4)
    ]
    half = requests // 2
    kept = lax.dynamic_slice_in_dim(tokens, half * group, half, 0)
    other = send(lax.dynamic_slice_in_dim(tokens, half * (1 - group), half, 0), "cfg", CFG_SWAP)
    owns = [
        jnp.concatenate([block[n * part : (n + 1) * part] for block in moved], axis=0)
        for n in range(CHUNKS)
    ]
    from_x = [[own] + [send(own, "tp", shift4(k)) for k in range(1, 4)] for own in owns]
    owns_later, pos_ids, mod_table = together(owns, pos_ids, mod_table)

    mine = [(z - owned_shard(group, z, i)) % 4 for i in range(2)]
    theirs = [(z - owned_shard(1 - group, z, i)) % 4 for i in range(2)]

    def some(array, which):
        return jnp.stack([pick(array.reshape(4, part, width), k) for k in which], axis=0)

    theirs_in = jnp.stack([some(own, theirs) for own in owns_later])
    modulation = pick(mod_table, pick(timestep, z))
    scale, shift = 1.0 + modulation[1:2], modulation[0:1]
    cosine, sine, w_qkv = rotary_tables(pos_ids, z, y, w_qkv)
    span = lambda v, n: v[n * rows : (n + 1) * rows]
    length = pick(text_len[0], z)

    gain_q, gain_k = qk_gain[0:1], qk_gain[1:2]
    wq = w_qkv[:, 0]
    wkv = w_qkv[:, 1:].reshape(D, 2 * inner)
    place = jnp.stack([z, y, length]).astype(jnp.int32)
    cosines = [span(cosine, n) for n in range(CHUNKS)]
    sines = [span(sine, n) for n in range(CHUNKS)]
    (from_x[0], wq, wkv, theirs_in, place, cosines, sines, order, near_order, far_order, scale, shift) = together(
        from_x[0], wq, wkv, theirs_in, place, cosines, sines, order, near_order, far_order, scale, shift
    )
    modded, kvs = [], []
    for n in range(CHUNKS):
        blocks = from_x[n]
        if n:
            blocks, kvs[n - 1] = together(blocks, kvs[n - 1])
        blocks = blocks + [send(block, "tp", SWAP) for block in blocks]
        m, kv = keys_values(
            order, blocks, scale, shift, wkv, gain_k, cosines[n], sines[n]
        )
        modded.append(m)
        kvs.append(kv)
    fars = [send(kvs[n], "seq", SWAP) for n in range(CHUNKS)]
    hidden_far = send(theirs_in, "cfg", CFG_SWAP)
    early = [
        queries_units(modded[n], wq, w_mlp, w_mlp_out, gain_q, cosines[n], sines[n])
        for n in range(CHUNKS)
    ]
    early, fars[-1] = together(early, fars[-1])
    kvs = kvs + fars

    peaks, joins = [], []
    for n in range(CHUNKS):
        queries, parts = early[n]
        if n:
            queries, joins[n - 1] = together(queries, joins[n - 1])
        attended, far_part, peak = attention(far_order, place, queries, kvs, w_attn_out, parts)
        peaks.append(peak[0:1])
        got = send(far_part, "tp", SWAP)
        joins.append(near_project(near_order, attended, w_attn_out, parts, got))
    landings = [[send(joins[n][k], "tp", shift4(k)) for k in range(1, 4)] for n in range(CHUNKS)]
    for n in range(CHUNKS - 1):
        landings[n], joins[n + 1] = together(landings[n], joins[n + 1])

    joins[-1], mod_gate, owns = together(joins[-1], modulation[2], owns)
    gate = lax.dynamic_slice_in_dim(mod_gate, tp * width, width, 0)
    own_square, raw_square, landings_home = f32(0), f32(0), []
    outgoing = change = None

    def home(change):
        return [send(change[i], ("cfg", "seq"), home_perm(i)) for i in range(2)]

    for n in range(CHUNKS):
        if n:
            outgoing, landings[n], joins[n] = together(outgoing, landings[n], joins[n])
        branch = joins[n][0]
        for arrived in landings[n]:
            branch = branch + arrived.astype(f32)
        delta = gate[None, :] * branch
        state = owns[n].astype(f32) + delta
        own_square = own_square + jnp.sum(state * state)
        outgoing = some(delta.astype(bf16), theirs)
        delta_far = send(outgoing, "cfg", CFG_SWAP).astype(f32)
        delta_near = some(delta, mine)
        near = some(owns[n], mine).astype(f32) + delta_near
        hidden = hidden_far[n]
        if n:
            hidden, change = together(hidden, change)
            landings_home.append(home(change))
        far = hidden.astype(f32) + delta_far
        conditional = jnp.where(group == 0, near, far)
        unconditional = jnp.where(group == 0, far, near)
        raw = unconditional + guidance_scale * (conditional - unconditional)
        raw_square = raw_square + jnp.sum(raw * raw)
        cond_delta = jnp.where(group == 0, delta_near, delta_far)
        free_delta = jnp.where(group == 0, delta_far, delta_near)
        change = (free_delta + guidance_scale * (cond_delta - free_delta)).astype(bf16)
    landings_home.append(home(change))
    lane = lax.broadcasted_iota(jnp.int32, (1, 128), 1)
    here = group * requests + z
    vector = jnp.where(lane < 12, 0.0, masked_value)
    vector = jnp.where(lane == here, own_square, vector)
    vector = jnp.where(lane == 8 + z, raw_square, vector)
    vector = jnp.where(lane == 12 + here, functools.reduce(jnp.maximum, peaks), vector)
    vector = reduce_all(vector, 12)[0]
    vector, landings_home = together(vector, landings_home)

    flip = (z % 2) ^ (z // 2) == 1
    changes = [
        jnp.stack([jnp.where(flip, landed[1 - i], landed[i]) for i in range(2)], axis=0)
        for landed in landings_home
    ]

    entries = float(SEQ_LEN * D)
    norm = jnp.sqrt(vector[:12] / entries + norm_eps)
    factors = rescale_share * norm[:4] / norm[8:] + (1.0 - rescale_share)
    factor = lax.dynamic_slice_in_dim(factors, half * group, half, 0)
    cond_in = jnp.where(group == 0, kept, other).astype(f32)
    free_in = jnp.where(group == 0, other, kept).astype(f32)
    base = free_in + guidance_scale * (cond_in - free_in)
    raw = base + jnp.concatenate(changes, axis=1).astype(f32)
    guided = (raw * factor[:, None, None]).astype(bf16)
    state_norm = lax.dynamic_slice_in_dim(norm, group * requests, requests, 0)
    max_logit = lax.dynamic_slice_in_dim(vector, 12 + group * requests, requests, 0)
    return (guided, state_norm[None, :], max_logit[None, :])


def solution(mesh):
    placed = (
        P("cfg", None, "seq", "tp"),
        P(None, None, "tp"),
        P(None, "tp"),
        P("tp", None),
        P("tp", None),
        P(),
        P(),
        P(),
        P("cfg", None),
        P(None, None, "seq"),
    )

    return jax.shard_map(
        local,
        mesh=mesh,
        in_specs=placed,
        out_specs=(P("cfg", "seq", "tp"), P("cfg", None), P("cfg", None)),
        check_vma=False,
    )
```

```python
import functools

import jax
import jax.numpy as jnp
from jax import lax
from jax.experimental import pallas as pl
from jax.experimental.pallas import tpu as pltpu
from jax.sharding import PartitionSpec as P


D = 3072
TXT = 512
SEQ_LEN = 1536
GRID = 32
HD = 128

norm_eps = 1e-06
rope_theta = 10000.0
guidance_scale = 4.0
rescale_share = 0.7
masked_value = -1e30

CHUNKS = 2


f32 = jnp.float32
bf16 = jnp.bfloat16

SWAP = [(i, i ^ 1) for i in range(8)]
CFG_SWAP = [(0, 1), (1, 0)]


def shift4(k):
    return [(i, ((i // 2 + k) % 4) * 2 + i % 2) for i in range(8)]


def owned_shard(g, z, i):
    return ((z + g) & 1) + 2 * (i ^ g)


def home_perm(i):
    return [
        (g * 8 + s, (s // 4) * 8 + owned_shard(g, s // 2, i) * 2 + s % 2)
        for g in range(2)
        for s in range(8)
    ]


def send(value, axes, pairs):
    return lax.ppermute(value, axes, pairs)


def together(*values):
    return lax.optimization_barrier(values)


def pick(array, index):
    return lax.dynamic_index_in_dim(array, index, 0, False)


VMEM = pl.BlockSpec(memory_space=pltpu.VMEM)
SMEM = pl.BlockSpec(memory_space=pltpu.SMEM)


HBM = pl.BlockSpec(memory_space=pltpu.HBM)


def call(kernel, outs, args, flops, specs, out_specs, scratch, grant):
    shapes = [jax.ShapeDtypeStruct(shape, dtype) for shape, dtype in outs]
    return pl.pallas_call(
        kernel,
        in_specs=specs,
        out_specs=out_specs,
        out_shape=shapes,
        scratch_shapes=scratch,
        compiler_params=pltpu.CompilerParams(vmem_limit_bytes=grant << 20),
        cost_estimate=pl.CostEstimate(
            flops=flops, transcendentals=0, bytes_accessed=sum(v.size * v.dtype.itemsize for v in args)
        ),
    )(*args)


def rotary(values, gain_row, cosine, sine, even):
    u = values * lax.rsqrt(jnp.mean(values * values, axis=-1, keepdims=True) + norm_eps) * gain_row
    turned = jnp.where(even, -pltpu.roll(u, HD - 1, 1), pltpu.roll(u, 1, 1))
    return u * cosine + turned * sine


def even_lanes(shape):
    return lax.broadcasted_iota(jnp.int32, shape, 1) % 2 == 0


LN_ROWS = 64
DOT_COLS = 256


def kv_kernel(order, *refs):
    blocks = refs[:8]
    scale_ref, shift_ref, w_ref, gain_ref, cos_ref, sin_ref, m_ref, kv_ref = refs[8:]
    rows, width = blocks[0].shape
    pieces = width // 128

    def norm(i, _):
        r = pl.ds(pl.multiple_of(i * LN_ROWS, LN_ROWS), LN_ROWS)

        def pieces_of(ref):
            return [ref[r, n * 128 : (n + 1) * 128].astype(f32) for n in range(pieces)]

        total = jnp.zeros((LN_ROWS, 128), f32)
        for ref in blocks:
            for v in pieces_of(ref):
                total = total + v
        mean = jnp.sum(total, axis=-1, keepdims=True) * (1.0 / D)
        square = jnp.zeros((LN_ROWS, 128), f32)
        for ref in blocks:
            for v in pieces_of(ref):
                center = v - mean
                square = square + center * center
        inverse = lax.rsqrt(jnp.sum(square, axis=-1, keepdims=True) * (1.0 / D) + norm_eps)
        for b, ref in enumerate(blocks):
            for n, v in enumerate(pieces_of(ref)):
                cols = pl.ds(pl.multiple_of(order[b] * width + n * 128, 128), 128)
                normed = (v - mean) * inverse
                m_ref[r, cols] = (scale_ref[:, cols] * normed + shift_ref[:, cols]).astype(bf16)
        return 0

    lax.fori_loop(0, rows // LN_ROWS, norm, 0)
    even = even_lanes((rows, HD))
    inner = w_ref.shape[1] // 2
    for n in range(w_ref.shape[1] // DOT_COLS):
        both = jnp.dot(
            m_ref[...], w_ref[:, n * DOT_COLS : (n + 1) * DOT_COLS], preferred_element_type=f32
        )
        for h in range(DOT_COLS // HD):
            v = both[:, h * HD : (h + 1) * HD]
            at = n * DOT_COLS + h * HD
            if at < inner:
                v = rotary(v, gain_ref[...], cos_ref[...], sin_ref[...], even)
            kv_ref[:, at : at + HD] = v.astype(bf16)


def keys_values(order, blocks, scale, shift, weight, gain, cosine, sine):
    rows = blocks[0].shape[0]
    args = (order, *blocks, scale, shift, weight, gain, cosine, sine)
    return call(
        kv_kernel,
        [((rows, D), bf16), ((rows, weight.shape[1]), bf16)],
        args,
        2 * rows * D * weight.shape[1],
        [SMEM] + [VMEM] * 14,
        [VMEM, VMEM],
        [],
        8,
    )


def qu_kernel(m_ref, wq_ref, wm_ref, wo_ref, gain_ref, cos_ref, sin_ref, q_ref, part_ref, u_ref):
    rows = m_ref.shape[0]
    even = even_lanes((rows, HD))
    for h in range(q_ref.shape[1] // HD):
        c = slice(h * HD, (h + 1) * HD)
        if h % 2 == 0:
            wide = slice(h * HD, min((h + 2) * HD, q_ref.shape[1]))
            pair = jnp.dot(m_ref[...], wq_ref[:, wide], preferred_element_type=f32)
        q = pair[:, (h % 2) * HD : (h % 2 + 1) * HD]
        q_ref[:, c] = rotary(q, gain_ref[...], cos_ref[...], sin_ref[...], even).astype(bf16)

    for n in range(wm_ref.shape[1] // DOT_COLS):
        c = slice(n * DOT_COLS, (n + 1) * DOT_COLS)
        u = jnp.dot(m_ref[...], wm_ref[:, c], preferred_element_type=f32)
        u_ref[:, c] = jax.nn.gelu(u, approximate=True).astype(bf16)

    def part(n, _):
        c = pl.ds(pl.multiple_of(n * DOT_COLS, DOT_COLS), DOT_COLS)
        part_ref[:, c] = jnp.dot(u_ref[...], wo_ref[:, c], preferred_element_type=f32)
        return 0

    lax.fori_loop(0, D // DOT_COLS, part, 0)


def queries_units(modded, wq, wm, wo, gain, cosine, sine):
    rows = modded.shape[0]
    inner, hidden = wq.shape[1], wm.shape[1]
    args = (modded, wq, wm, wo, gain, cosine, sine)
    return call(
        qu_kernel,
        [((rows, inner), bf16), ((rows, D), f32)],
        args,
        2 * rows * D * (inner + 2 * hidden),
        [VMEM] * 7,
        [VMEM] * 2,
        [pltpu.VMEM((rows, hidden), bf16)],
        8,
    )


Q_ROWS = 192
LOG2E = 1.4426950408889634


def attention_kernel(order, place, q_ref, *refs):
    kvs = refs[:4]
    w_ref, part_ref, o_ref, far_ref, peak_ref = refs[4:]
    rows, inner = o_ref.shape
    width = far_ref.shape[2]
    piece = rows // 4
    z, y, length = place[0], place[1], place[2]
    lane = lax.broadcasted_iota(jnp.int32, (1, rows), 1)
    block = sum((lane >= k * piece).astype(jnp.int32) for k in range(1, 4))
    biases = []
    for n in range(4):
        shard = 2 * ((z - block) & 3) + (y if n < 2 else 1 - y)
        position = shard * (2 * piece) + (n % 2) * piece + lane - block * piece
        usable = (position >= TXT) | (position < length)
        biases.append(jnp.where(usable, 0.0, masked_value).astype(f32))
    contract = (((1,), (1,)), ((), ()))
    scale = HD ** (-0.5)

    def tile(i, top):
        r = pl.ds(pl.multiple_of(i * Q_ROWS, Q_ROWS), Q_ROWS)
        for h in range(inner // HD):
            c = slice(h * HD, (h + 1) * HD)
            cv = slice(inner + h * HD, inner + (h + 1) * HD)
            q = q_ref[r, c]
            logits = [
                lax.dot_general(q, kv[:, c], contract, preferred_element_type=f32) + bias
                for kv, bias in zip(kvs, biases)
            ]
            peak = functools.reduce(jnp.maximum, [jnp.max(s, axis=-1, keepdims=True) for s in logits])
            total, mix = None, None
            for kv, s in zip(kvs, logits):
                w = jnp.exp2((s - peak) * (scale * LOG2E))
                part = jnp.sum(w, axis=-1, keepdims=True)
                prod = jnp.dot(w.astype(bf16), kv[:, cv], preferred_element_type=f32)
                total = part if total is None else total + part
                mix = prod if mix is None else mix + prod
            o_ref[r, c] = (mix / total).astype(bf16)
            top = jnp.maximum(top, jnp.max(peak))
        return top

    top = lax.fori_loop(0, rows // Q_ROWS, tile, f32(masked_value))
    peak_ref[...] = jnp.full(peak_ref.shape, top * scale, f32)
    for n in range(4):
        cols = pl.ds(pl.multiple_of(order[n] * width, 128), width)
        far_ref[n] = (
            part_ref[:, cols] + jnp.dot(o_ref[...], w_ref[:, cols], preferred_element_type=f32)
        ).astype(bf16)


def attention(order, place, q, kvs, w_attn_out, parts):
    rows, inner = q.shape
    args = (order, place, q, *kvs, w_attn_out, parts)
    return call(
        attention_kernel,
        [((rows, inner), bf16), ((4, rows, D // 8), bf16), ((8, 128), f32)],
        args,
        24 * rows * rows * inner,
        [SMEM] * 2 + [VMEM] * 7,
        [VMEM] * 3,
        [],
        8,
    )


def near_kernel(order, a_ref, w_ref, part_ref, got_ref, *out_refs):
    width = got_ref.shape[2]
    for n, o_ref in enumerate(out_refs):
        cols = pl.ds(pl.multiple_of(order[n] * width, 128), width)
        total = part_ref[:, cols] + jnp.dot(a_ref[...], w_ref[:, cols], preferred_element_type=f32)
        o_ref[...] = (total + got_ref[n].astype(f32)).astype(o_ref.dtype)


def near_project(order, attended, w_attn_out, parts, got):
    rows, inner = attended.shape
    return call(
        near_kernel,
        [((rows, D // 8), f32)] + [((rows, D // 8), bf16)] * 3,
        (order, attended, w_attn_out, parts, got),
        rows * inner * D,
        [SMEM] + [VMEM] * 4,
        [VMEM] * 4,
        [],
        8,
    )


def rotary_tables(pos_ids, z, y, w_qkv):
    local_len = pos_ids.shape[2]
    image = (2 * z + y) * local_len + jnp.arange(local_len, dtype=jnp.int32) - TXT
    is_image = (image >= 0)[None, :]
    row_offset = jnp.max(jnp.where(is_image, pos_ids[:, 1] - (image // GRID)[None, :], -1), axis=1)
    col_offset = jnp.max(jnp.where(is_image, pos_ids[:, 2] - (image % GRID)[None, :], -1), axis=1)
    mine = jnp.stack([row_offset, col_offset], axis=0)
    above = send(mine, "seq", shift4(3))
    above, w_qkv = together(above, w_qkv)
    offsets = jnp.where(z == 0, above, mine)
    offsets = lax.dynamic_index_in_dim(offsets, z, 1, False)
    blocks = jnp.arange(4, dtype=jnp.int32)
    shard = 2 * ((z - blocks) & 3) + y
    part = local_len // CHUNKS
    start = jnp.arange(CHUNKS, dtype=jnp.int32)[:, None, None] * part + jnp.arange(part, dtype=jnp.int32)
    position = (shard[None, :, None] * local_len + start).reshape(-1)
    index = position - TXT
    pair_index = jnp.arange(HD, dtype=jnp.int32) // 2
    first_end = HD // 16
    second = first_end + (HD - HD // 8) // 4
    axis_of = jnp.where(pair_index < first_end, 0, jnp.where(pair_index < second, 1, 2))
    start = jnp.where(axis_of == 0, 0, jnp.where(axis_of == 1, first_end, second))
    span = jnp.where(axis_of == 0, HD // 8, (HD - HD // 8) // 2)
    frequency = jnp.power(f32(rope_theta), -2.0 * (pair_index - start).astype(f32) / span.astype(f32))
    row_id = jnp.where(index >= 0, index // GRID + offsets[0], 0).astype(f32)
    col_id = jnp.where(index >= 0, index % GRID + offsets[1], 0).astype(f32)
    angles = row_id[:, None] * jnp.where(axis_of == 1, frequency, 0.0)[None, :]
    angles = angles + col_id[:, None] * jnp.where(axis_of == 2, frequency, 0.0)[None, :]
    return jnp.cos(angles), jnp.sin(angles), w_qkv


def reduce_all(vector, sums):
    lane = lax.broadcasted_iota(jnp.int32, vector.shape, 1)
    every = jnp.broadcast_to(vector[None], (128,) + vector.shape)
    every = lax.all_to_all(every, ("cfg", "seq", "tp"), 0, 0, tiled=True)
    return jnp.where(lane < sums, jnp.sum(every, axis=0), jnp.max(every, axis=0))


def local(
    hidden_in, w_qkv, w_mlp, w_attn_out, w_mlp_out, mod_table, qk_gain, timestep, text_len, pos_ids
):
    tokens = hidden_in[0]
    requests, local_len, width = tokens.shape
    inner = w_qkv.shape[2]
    group = lax.axis_index("cfg")
    seq = lax.axis_index("seq")
    z, y = seq >> 1, seq & 1
    tp = lax.axis_index("tp")
    x, core = tp >> 1, tp & 1

    part = local_len // CHUNKS
    rows = 4 * part
    steps = jnp.arange(4, dtype=jnp.int32)
    back = 2 * ((x - steps) & 3)
    order = jnp.concatenate([back + core, back + 1 - core]).astype(jnp.int32)
    ahead = 2 * ((x + steps) & 3)
    near_order = (ahead + core).astype(jnp.int32)
    far_order = (ahead + 1 - core).astype(jnp.int32)

    moved = [pick(tokens, z)] + [
        send(pick(tokens, (z + k) & 3), "seq", shift4(k)) for k in range(1, 4)
    ]
    owns = [
        jnp.concatenate([block[n * part : (n + 1) * part] for block in moved], axis=0)
        for n in range(CHUNKS)
    ]
    from_x = [[own] + [send(own, "tp", shift4(k)) for k in range(1, 4)] for own in owns]
    owns_later, pos_ids, mod_table = together(owns, pos_ids, mod_table)

    mine = [(z - owned_shard(group, z, i)) & 3 for i in range(2)]
    theirs = [(z - owned_shard(1 - group, z, i)) & 3 for i in range(2)]

    def some(array, which):
        return jnp.stack([pick(array.reshape(4, part, width), k) for k in which], axis=0)

    modulation = pick(mod_table, pick(timestep, z))
    scale, shift = 1.0 + modulation[1:2], modulation[0:1]
    cosine, sine, w_qkv = rotary_tables(pos_ids, z, y, w_qkv)
    span = lambda v, n: v[n * rows : (n + 1) * rows]
    length = pick(text_len[0], z)

    gain_q, gain_k = qk_gain[0:1], qk_gain[1:2]
    wq = w_qkv[:, 0]
    wkv = w_qkv[:, 1:].reshape(D, 2 * inner)
    place = jnp.stack([z, y, length]).astype(jnp.int32)
    cosines = [span(cosine, n) for n in range(CHUNKS)]
    sines = [span(sine, n) for n in range(CHUNKS)]
    (from_x[0], wq, wkv, place, cosines, sines, order, near_order, far_order, scale, shift) = together(
        from_x[0], wq, wkv, place, cosines, sines, order, near_order, far_order, scale, shift
    )
    modded, kvs = [], []
    for n in range(CHUNKS):
        blocks = from_x[n]
        if n:
            blocks, kvs[n - 1] = together(blocks, kvs[n - 1])
        blocks = blocks + [send(block, "tp", SWAP) for block in blocks]
        m, kv = keys_values(
            order, blocks, scale, shift, wkv, gain_k, cosines[n], sines[n]
        )
        modded.append(m)
        kvs.append(kv)
    fars = [send(kvs[n], "seq", SWAP) for n in range(CHUNKS)]
    early = [
        queries_units(modded[n], wq, w_mlp, w_mlp_out, gain_q, cosines[n], sines[n])
        for n in range(CHUNKS)
    ]
    early, fars[-1] = together(early, fars[-1])
    kvs = kvs + fars

    peaks, joins = [], []
    for n in range(CHUNKS):
        queries, parts = early[n]
        if n:
            queries, joins[n - 1] = together(queries, joins[n - 1])
        attended, far_part, peak = attention(far_order, place, queries, kvs, w_attn_out, parts)
        peaks.append(peak[0:1])
        got = send(far_part, "tp", SWAP)
        if n == 0:
            owns_late, far_part = together(owns_later, far_part)
            theirs_in = jnp.stack([some(own, theirs) for own in owns_late])
        joins.append(near_project(near_order, attended, w_attn_out, parts, got))
    half = requests // 2
    tokens, joins[0] = together(tokens, joins[0])
    hidden_far = send(theirs_in, "cfg", CFG_SWAP)
    other = send(lax.dynamic_slice_in_dim(tokens, half * (1 - group), half, 0), "cfg", CFG_SWAP)
    landings = [[send(joins[n][k], "tp", shift4(k)) for k in range(1, 4)] for n in range(CHUNKS)]
    for n in range(CHUNKS - 1):
        landings[n], joins[n + 1] = together(landings[n], joins[n + 1])

    joins[-1], modulation, owns, tokens = together(joins[-1], modulation, owns, tokens)
    kept = lax.dynamic_slice_in_dim(tokens, half * group, half, 0)
    gate = lax.dynamic_slice(modulation, (2, tp * width), (1, width))
    own_square, raw_square, changes = f32(0), f32(0), []
    outgoing = change = None

    for n in range(CHUNKS):
        if n:
            outgoing, landings[n], joins[n], other = together(outgoing, landings[n], joins[n], other)
        branch = joins[n][0]
        for arrived in landings[n]:
            branch = branch + arrived.astype(f32)
        delta = gate * branch
        state = owns[n].astype(f32) + delta
        own_square = own_square + jnp.sum(state * state)
        outgoing = some(delta.astype(bf16), theirs)
        delta_far = send(outgoing, "cfg", CFG_SWAP)
        if n == 0:
            delta_far, hidden_far = together(delta_far, hidden_far)
        delta_far = delta_far.astype(f32)
        delta_near = some(delta, mine)
        near = some(owns[n], mine).astype(f32) + delta_near
        hidden = hidden_far[n]
        if n:
            hidden, change = together(hidden, change)
            changes.append(change)
        far = hidden.astype(f32) + delta_far
        conditional = jnp.where(group == 0, near, far)
        unconditional = jnp.where(group == 0, far, near)
        raw = unconditional + guidance_scale * (conditional - unconditional)
        raw_square = raw_square + jnp.sum(raw * raw)
        cond_delta = jnp.where(group == 0, delta_near, delta_far)
        free_delta = jnp.where(group == 0, delta_far, delta_near)
        change = (free_delta + guidance_scale * (cond_delta - free_delta)).astype(bf16)
    changes.append(change)
    landed = [
        send(jnp.stack([c[i] for c in changes]), ("cfg", "seq"), home_perm(i)) for i in range(2)
    ]
    lane = lax.broadcasted_iota(jnp.int32, (1, 128), 1)
    here = group * requests + z
    vector = jnp.where(lane < 12, 0.0, masked_value)
    vector = jnp.where(lane == here, own_square, vector)
    vector = jnp.where(lane == 8 + z, raw_square, vector)
    vector = jnp.where(lane == 12 + here, functools.reduce(jnp.maximum, peaks), vector)
    vector = reduce_all(vector, 12)[0]
    vector, landed = together(vector, landed)

    flip = (z & 1) ^ (z >> 1) == 1
    change = jnp.stack([jnp.where(flip, landed[1 - i], landed[i]) for i in range(2)], axis=0)
    change = change.reshape(half, local_len, width).astype(f32)
    entries = float(SEQ_LEN * D)
    norm = jnp.sqrt(vector[:12] / entries + norm_eps)
    factors = rescale_share * norm[:4] / norm[8:] + (1.0 - rescale_share)
    factor = lax.dynamic_slice_in_dim(factors, half * group, half, 0)
    cond_in = jnp.where(group == 0, kept, other).astype(f32)
    free_in = jnp.where(group == 0, other, kept).astype(f32)
    base = free_in + guidance_scale * (cond_in - free_in)
    raw = base + change
    guided = (raw * factor[:, None, None]).astype(bf16)
    state_norm = lax.dynamic_slice_in_dim(norm, group * requests, requests, 0)
    max_logit = lax.dynamic_slice_in_dim(vector, 12 + group * requests, requests, 0)
    return (guided, state_norm[None, :], max_logit[None, :])


def solution(mesh):
    placed = (
        P("cfg", None, "seq", "tp"),
        P(None, None, "tp"),
        P(None, "tp"),
        P("tp", None),
        P("tp", None),
        P(),
        P(),
        P(),
        P("cfg", None),
        P(None, None, "seq"),
    )

    return jax.shard_map(
        local,
        mesh=mesh,
        in_specs=placed,
        out_specs=(P("cfg", "seq", "tp"), P("cfg", None), P("cfg", None)),
        check_vma=False,
    )
```

```python
import functools

import jax
import jax.numpy as jnp
from jax import lax
from jax.experimental import pallas as pl
from jax.experimental.pallas import tpu as pltpu
from jax.sharding import PartitionSpec as P


D = 3072
TXT = 512
SEQ_LEN = 1536
GRID = 32
HD = 128

norm_eps = 1e-06
rope_theta = 10000.0
guidance_scale = 4.0
rescale_share = 0.7
masked_value = -1e30

CHUNKS = 2


f32 = jnp.float32
bf16 = jnp.bfloat16

SWAP = [(i, i ^ 1) for i in range(8)]
CFG_SWAP = [(0, 1), (1, 0)]


def shift4(k):
    return [(i, ((i // 2 + k) % 4) * 2 + i % 2) for i in range(8)]


def owned_shard(g, z, i):
    return ((z + g) & 1) + 2 * (i ^ g)


def home_perm(i):
    return [
        (g * 8 + s, (s // 4) * 8 + owned_shard(g, s // 2, i) * 2 + s % 2)
        for g in range(2)
        for s in range(8)
    ]


def send(value, axes, pairs):
    return lax.ppermute(value, axes, pairs)


def together(*values):
    return lax.optimization_barrier(values)


def pick(array, index):
    return lax.dynamic_index_in_dim(array, index, 0, False)


VMEM = pl.BlockSpec(memory_space=pltpu.VMEM)
SMEM = pl.BlockSpec(memory_space=pltpu.SMEM)


HBM = pl.BlockSpec(memory_space=pltpu.HBM)


def call(kernel, outs, args, flops, specs, out_specs, scratch, grant):
    shapes = [jax.ShapeDtypeStruct(shape, dtype) for shape, dtype in outs]
    return pl.pallas_call(
        kernel,
        in_specs=specs,
        out_specs=out_specs,
        out_shape=shapes,
        scratch_shapes=scratch,
        compiler_params=pltpu.CompilerParams(vmem_limit_bytes=grant << 20),
        cost_estimate=pl.CostEstimate(
            flops=flops, transcendentals=0, bytes_accessed=sum(v.size * v.dtype.itemsize for v in args)
        ),
    )(*args)


def rotary(values, gain_row, cosine, sine, even):
    u = values * lax.rsqrt(jnp.mean(values * values, axis=-1, keepdims=True) + norm_eps) * gain_row
    turned = jnp.where(even, -pltpu.roll(u, HD - 1, 1), pltpu.roll(u, 1, 1))
    return u * cosine + turned * sine


def even_lanes(shape):
    return lax.broadcasted_iota(jnp.int32, shape, 1) % 2 == 0


LN_ROWS = 64
DOT_COLS = 256


def kv_kernel(order, *refs):
    blocks = refs[:8]
    scale_ref, shift_ref, w_ref, gain_ref, cos_ref, sin_ref, m_ref, kv_ref = refs[8:]
    rows, width = blocks[0].shape
    pieces = width // 128

    def norm(i, _):
        r = pl.ds(pl.multiple_of(i * LN_ROWS, LN_ROWS), LN_ROWS)

        def pieces_of(ref):
            return [ref[r, n * 128 : (n + 1) * 128].astype(f32) for n in range(pieces)]

        total = jnp.zeros((LN_ROWS, 128), f32)
        for ref in blocks:
            for v in pieces_of(ref):
                total = total + v
        mean = jnp.sum(total, axis=-1, keepdims=True) * (1.0 / D)
        square = jnp.zeros((LN_ROWS, 128), f32)
        for ref in blocks:
            for v in pieces_of(ref):
                center = v - mean
                square = square + center * center
        inverse = lax.rsqrt(jnp.sum(square, axis=-1, keepdims=True) * (1.0 / D) + norm_eps)
        for b, ref in enumerate(blocks):
            for n, v in enumerate(pieces_of(ref)):
                cols = pl.ds(pl.multiple_of(order[b] * width + n * 128, 128), 128)
                normed = (v - mean) * inverse
                m_ref[r, cols] = (scale_ref[:, cols] * normed + shift_ref[:, cols]).astype(bf16)
        return 0

    lax.fori_loop(0, rows // LN_ROWS, norm, 0)
    even = even_lanes((rows, HD))
    inner = w_ref.shape[1] // 2
    for n in range(w_ref.shape[1] // DOT_COLS):
        both = jnp.dot(
            m_ref[...], w_ref[:, n * DOT_COLS : (n + 1) * DOT_COLS], preferred_element_type=f32
        )
        for h in range(DOT_COLS // HD):
            v = both[:, h * HD : (h + 1) * HD]
            at = n * DOT_COLS + h * HD
            if at < inner:
                v = rotary(v, gain_ref[...], cos_ref[...], sin_ref[...], even)
            kv_ref[:, at : at + HD] = v.astype(bf16)


def keys_values(order, blocks, scale, shift, weight, gain, cosine, sine):
    rows = blocks[0].shape[0]
    args = (order, *blocks, scale, shift, weight, gain, cosine, sine)
    return call(
        kv_kernel,
        [((rows, D), bf16), ((rows, weight.shape[1]), bf16)],
        args,
        2 * rows * D * weight.shape[1],
        [SMEM] + [VMEM] * 14,
        [VMEM, VMEM],
        [],
        8,
    )


def qu_kernel(m_ref, wq_ref, wm_ref, wo_ref, gain_ref, cos_ref, sin_ref, q_ref, part_ref, u_ref):
    rows = m_ref.shape[0]
    even = even_lanes((rows, HD))
    for h in range(q_ref.shape[1] // HD):
        c = slice(h * HD, (h + 1) * HD)
        if h % 2 == 0:
            wide = slice(h * HD, min((h + 2) * HD, q_ref.shape[1]))
            pair = jnp.dot(m_ref[...], wq_ref[:, wide], preferred_element_type=f32)
        q = pair[:, (h % 2) * HD : (h % 2 + 1) * HD]
        q_ref[:, c] = rotary(q, gain_ref[...], cos_ref[...], sin_ref[...], even).astype(bf16)

    for n in range(wm_ref.shape[1] // DOT_COLS):
        c = slice(n * DOT_COLS, (n + 1) * DOT_COLS)
        u = jnp.dot(m_ref[...], wm_ref[:, c], preferred_element_type=f32)
        u_ref[:, c] = jax.nn.gelu(u, approximate=True).astype(bf16)

    def part(n, _):
        c = pl.ds(pl.multiple_of(n * DOT_COLS, DOT_COLS), DOT_COLS)
        part_ref[:, c] = jnp.dot(u_ref[...], wo_ref[:, c], preferred_element_type=f32)
        return 0

    lax.fori_loop(0, D // DOT_COLS, part, 0)


def queries_units(modded, wq, wm, wo, gain, cosine, sine):
    rows = modded.shape[0]
    inner, hidden = wq.shape[1], wm.shape[1]
    args = (modded, wq, wm, wo, gain, cosine, sine)
    return call(
        qu_kernel,
        [((rows, inner), bf16), ((rows, D), f32)],
        args,
        2 * rows * D * (inner + 2 * hidden),
        [VMEM] * 7,
        [VMEM] * 2,
        [pltpu.VMEM((rows, hidden), bf16)],
        8,
    )


Q_ROWS = 192
LOG2E = 1.4426950408889634


def attention_kernel(order, place, q_ref, *refs):
    kvs = refs[:4]
    w_ref, part_ref, o_ref, far_ref, peak_ref = refs[4:]
    rows, inner = o_ref.shape
    width = far_ref.shape[2]
    piece = rows // 4
    z, y, length = place[0], place[1], place[2]
    lane = lax.broadcasted_iota(jnp.int32, (1, rows), 1)
    block = sum((lane >= k * piece).astype(jnp.int32) for k in range(1, 4))
    biases = []
    for n in range(4):
        shard = 2 * ((z - block) & 3) + (y if n < 2 else 1 - y)
        position = shard * (2 * piece) + (n % 2) * piece + lane - block * piece
        usable = (position >= TXT) | (position < length)
        biases.append(jnp.where(usable, 0.0, masked_value).astype(f32))
    contract = (((1,), (1,)), ((), ()))
    scale = HD ** (-0.5)

    def tile(i, top):
        r = pl.ds(pl.multiple_of(i * Q_ROWS, Q_ROWS), Q_ROWS)
        for h in range(inner // HD):
            c = slice(h * HD, (h + 1) * HD)
            cv = slice(inner + h * HD, inner + (h + 1) * HD)
            q = q_ref[r, c]
            logits = [
                lax.dot_general(q, kv[:, c], contract, preferred_element_type=f32) + bias
                for kv, bias in zip(kvs, biases)
            ]
            peak = functools.reduce(jnp.maximum, [jnp.max(s, axis=-1, keepdims=True) for s in logits])
            total, mix = None, None
            for kv, s in zip(kvs, logits):
                w = jnp.exp2((s - peak) * (scale * LOG2E))
                part = jnp.sum(w, axis=-1, keepdims=True)
                prod = jnp.dot(w.astype(bf16), kv[:, cv], preferred_element_type=f32)
                total = part if total is None else total + part
                mix = prod if mix is None else mix + prod
            o_ref[r, c] = (mix / total).astype(bf16)
            top = jnp.maximum(top, jnp.max(peak))
        return top

    top = lax.fori_loop(0, rows // Q_ROWS, tile, f32(masked_value))
    peak_ref[...] = jnp.full(peak_ref.shape, top * scale, f32)
    for n in range(4):
        cols = pl.ds(pl.multiple_of(order[n] * width, 128), width)
        far_ref[n] = (
            part_ref[:, cols] + jnp.dot(o_ref[...], w_ref[:, cols], preferred_element_type=f32)
        ).astype(bf16)


def attention(order, place, q, kvs, w_attn_out, parts):
    rows, inner = q.shape
    args = (order, place, q, *kvs, w_attn_out, parts)
    return call(
        attention_kernel,
        [((rows, inner), bf16), ((4, rows, D // 8), bf16), ((8, 128), f32)],
        args,
        24 * rows * rows * inner,
        [SMEM] * 2 + [VMEM] * 7,
        [VMEM] * 3,
        [],
        8,
    )


def near_kernel(order, a_ref, w_ref, part_ref, got_ref, *out_refs):
    width = got_ref.shape[2]
    for n, o_ref in enumerate(out_refs):
        cols = pl.ds(pl.multiple_of(order[n] * width, 128), width)
        total = part_ref[:, cols] + jnp.dot(a_ref[...], w_ref[:, cols], preferred_element_type=f32)
        o_ref[...] = (total + got_ref[n].astype(f32)).astype(o_ref.dtype)


def near_project(order, attended, w_attn_out, parts, got):
    rows, inner = attended.shape
    return call(
        near_kernel,
        [((rows, D // 8), f32)] + [((rows, D // 8), bf16)] * 3,
        (order, attended, w_attn_out, parts, got),
        rows * inner * D,
        [SMEM] + [VMEM] * 4,
        [VMEM] * 4,
        [],
        8,
    )


def rotary_tables(pos_ids, z, y, w_qkv):
    local_len = pos_ids.shape[2]
    image = (2 * z + y) * local_len + jnp.arange(local_len, dtype=jnp.int32) - TXT
    is_image = (image >= 0)[None, :]
    row_offset = jnp.max(jnp.where(is_image, pos_ids[:, 1] - (image // GRID)[None, :], -1), axis=1)
    col_offset = jnp.max(jnp.where(is_image, pos_ids[:, 2] - (image % GRID)[None, :], -1), axis=1)
    mine = jnp.stack([row_offset, col_offset], axis=0)
    above = send(mine, "seq", shift4(3))
    above, w_qkv = together(above, w_qkv)
    offsets = jnp.where(z == 0, above, mine)
    offsets = lax.dynamic_index_in_dim(offsets, z, 1, False)
    blocks = jnp.arange(4, dtype=jnp.int32)
    shard = 2 * ((z - blocks) & 3) + y
    part = local_len // CHUNKS
    start = jnp.arange(CHUNKS, dtype=jnp.int32)[:, None, None] * part + jnp.arange(part, dtype=jnp.int32)
    position = (shard[None, :, None] * local_len + start).reshape(-1)
    index = position - TXT
    pair_index = jnp.arange(HD, dtype=jnp.int32) // 2
    first_end = HD // 16
    second = first_end + (HD - HD // 8) // 4
    axis_of = jnp.where(pair_index < first_end, 0, jnp.where(pair_index < second, 1, 2))
    start = jnp.where(axis_of == 0, 0, jnp.where(axis_of == 1, first_end, second))
    span = jnp.where(axis_of == 0, HD // 8, (HD - HD // 8) // 2)
    frequency = jnp.power(f32(rope_theta), -2.0 * (pair_index - start).astype(f32) / span.astype(f32))
    row_id = jnp.where(index >= 0, index // GRID + offsets[0], 0).astype(f32)
    col_id = jnp.where(index >= 0, index % GRID + offsets[1], 0).astype(f32)
    angles = row_id[:, None] * jnp.where(axis_of == 1, frequency, 0.0)[None, :]
    angles = angles + col_id[:, None] * jnp.where(axis_of == 2, frequency, 0.0)[None, :]
    return jnp.cos(angles), jnp.sin(angles), w_qkv, above


def reduce_all(vector, sums):
    lane = lax.broadcasted_iota(jnp.int32, vector.shape, 1)
    every = jnp.broadcast_to(vector[None], (128,) + vector.shape)
    every = lax.all_to_all(every, ("cfg", "seq", "tp"), 0, 0, tiled=True)
    return jnp.where(lane < sums, jnp.sum(every, axis=0), jnp.max(every, axis=0))


def local(
    hidden_in, w_qkv, w_mlp, w_attn_out, w_mlp_out, mod_table, qk_gain, timestep, text_len, pos_ids
):
    tokens = hidden_in[0]
    requests, local_len, width = tokens.shape
    inner = w_qkv.shape[2]
    group = lax.axis_index("cfg")
    seq = lax.axis_index("seq")
    z, y = seq >> 1, seq & 1
    tp = lax.axis_index("tp")
    x, core = tp >> 1, tp & 1

    part = local_len // CHUNKS
    rows = 4 * part
    steps = jnp.arange(4, dtype=jnp.int32)
    back = 2 * ((x - steps) & 3)
    order = jnp.concatenate([back + core, back + 1 - core]).astype(jnp.int32)
    ahead = 2 * ((x + steps) & 3)
    near_order = (ahead + core).astype(jnp.int32)
    far_order = (ahead + 1 - core).astype(jnp.int32)

    moved = [pick(tokens, z)] + [
        send(pick(tokens, (z + k) & 3), "seq", shift4(k)) for k in range(1, 4)
    ]
    owns = [
        jnp.concatenate([block[n * part : (n + 1) * part] for block in moved], axis=0)
        for n in range(CHUNKS)
    ]
    from_x = [[own] + [send(own, "tp", shift4(k)) for k in range(1, 4)] for own in owns]
    owns_later, pos_ids, mod_table = together(owns, pos_ids, mod_table)

    mine = [(z - owned_shard(group, z, i)) & 3 for i in range(2)]
    theirs = [(z - owned_shard(1 - group, z, i)) & 3 for i in range(2)]

    def some(array, which):
        return jnp.stack([pick(array.reshape(4, part, width), k) for k in which], axis=0)

    modulation = pick(mod_table, pick(timestep, z))
    scale, shift = 1.0 + modulation[1:2], modulation[0:1]
    cosine, sine, w_qkv, above = rotary_tables(pos_ids, z, y, w_qkv)
    span = lambda v, n: v[n * rows : (n + 1) * rows]
    length = pick(text_len[0], z)

    gain_q, gain_k = qk_gain[0:1], qk_gain[1:2]
    wkv = w_qkv[:, 1:].reshape(D, 2 * inner)
    half = requests // 2
    theirs_in = jnp.stack([some(own, theirs) for own in owns_later])
    tokens, above = together(tokens, above)
    other_in = lax.dynamic_slice_in_dim(tokens, half * (1 - group), half, 0)
    place = jnp.stack([z, y, length]).astype(jnp.int32)
    cosines = [span(cosine, n) for n in range(CHUNKS)]
    sines = [span(sine, n) for n in range(CHUNKS)]
    (from_x[0], wkv, theirs_in, other_in, place, cosines, sines, order, near_order, far_order, scale, shift) = together(
        from_x[0], wkv, theirs_in, other_in, place, cosines, sines, order, near_order, far_order, scale, shift
    )
    modded, kvs = [], []
    for n in range(CHUNKS):
        blocks = from_x[n]
        if n:
            blocks, kvs[n - 1] = together(blocks, kvs[n - 1])
        blocks = blocks + [send(block, "tp", SWAP) for block in blocks]
        m, kv = keys_values(
            order, blocks, scale, shift, wkv, gain_k, cosines[n], sines[n]
        )
        modded.append(m)
        kvs.append(kv)
    w_qkv, kvs[-1] = together(w_qkv, kvs[-1])
    wq = w_qkv[:, 0]
    fars = [send(kvs[n], "seq", SWAP) for n in range(CHUNKS)]
    early = [
        queries_units(modded[n], wq, w_mlp, w_mlp_out, gain_q, cosines[n], sines[n])
        for n in range(CHUNKS)
    ]
    early, fars[-1] = together(early, fars[-1])
    kvs = kvs + fars

    peaks, joins = [], []
    for n in range(CHUNKS):
        queries, parts = early[n]
        if n:
            queries, joins[n - 1] = together(queries, joins[n - 1])
        attended, far_part, peak = attention(far_order, place, queries, kvs, w_attn_out, parts)
        peaks.append(peak[0:1])
        got = send(far_part, "tp", SWAP)
        joins.append(near_project(near_order, attended, w_attn_out, parts, got))
    hidden_far = send(theirs_in, "cfg", CFG_SWAP)
    other = send(other_in, "cfg", CFG_SWAP)
    landings = [[send(joins[n][k], "tp", shift4(k)) for k in range(1, 4)] for n in range(CHUNKS)]
    for n in range(CHUNKS - 1):
        landings[n], joins[n + 1] = together(landings[n], joins[n + 1])

    joins[-1], mod_table, owns, tokens = together(joins[-1], mod_table, owns, tokens)
    kept = lax.dynamic_slice_in_dim(tokens, half * group, half, 0)
    gate = lax.dynamic_slice(mod_table, (pick(timestep, z), 2, tp * width), (1, 1, width))[0]
    own_square, raw_square, changes = f32(0), f32(0), []
    outgoing = change = None

    for n in range(CHUNKS):
        if n:
            outgoing, landings[n], joins[n] = together(outgoing, landings[n], joins[n])
        branch = joins[n][0]
        for arrived in landings[n]:
            branch = branch + arrived.astype(f32)
        delta = gate * branch
        state = owns[n].astype(f32) + delta
        own_square = own_square + jnp.sum(state * state)
        outgoing = some(delta.astype(bf16), theirs)
        delta_far = send(outgoing, "cfg", CFG_SWAP)
        if n == 0:
            delta_far, hidden_far = together(delta_far, hidden_far)
        delta_far = delta_far.astype(f32)
        delta_near = some(delta, mine)
        near = some(owns[n], mine).astype(f32) + delta_near
        hidden = hidden_far[n]
        if n:
            hidden, change = together(hidden, change)
            changes.append(change)
        far = hidden.astype(f32) + delta_far
        conditional = jnp.where(group == 0, near, far)
        unconditional = jnp.where(group == 0, far, near)
        raw = unconditional + guidance_scale * (conditional - unconditional)
        raw_square = raw_square + jnp.sum(raw * raw)
        cond_delta = jnp.where(group == 0, delta_near, delta_far)
        free_delta = jnp.where(group == 0, delta_far, delta_near)
        change = (free_delta + guidance_scale * (cond_delta - free_delta)).astype(bf16)
    changes.append(change)
    landed = [
        send(jnp.stack([c[i] for c in changes]), ("cfg", "seq"), home_perm(i)) for i in range(2)
    ]
    lane = lax.broadcasted_iota(jnp.int32, (1, 128), 1)
    here = group * requests + z
    vector = jnp.where(lane < 12, 0.0, masked_value)
    vector = jnp.where(lane == here, own_square, vector)
    vector = jnp.where(lane == 8 + z, raw_square, vector)
    vector = jnp.where(lane == 12 + here, functools.reduce(jnp.maximum, peaks), vector)
    vector = reduce_all(vector, 12)[0]
    vector, landed, other = together(vector, landed, other)

    flip = (z & 1) ^ (z >> 1) == 1
    change = jnp.stack([jnp.where(flip, landed[1 - i], landed[i]) for i in range(2)], axis=0)
    change = change.reshape(half, local_len, width).astype(f32)
    entries = float(SEQ_LEN * D)
    norm = jnp.sqrt(vector[:12] / entries + norm_eps)
    factors = rescale_share * norm[:4] / norm[8:] + (1.0 - rescale_share)
    factor = lax.dynamic_slice_in_dim(factors, half * group, half, 0)
    cond_in = jnp.where(group == 0, kept, other).astype(f32)
    free_in = jnp.where(group == 0, other, kept).astype(f32)
    base = free_in + guidance_scale * (cond_in - free_in)
    raw = base + change
    guided = (raw * factor[:, None, None]).astype(bf16)
    state_norm = lax.dynamic_slice_in_dim(norm, group * requests, requests, 0)
    max_logit = lax.dynamic_slice_in_dim(vector, 12 + group * requests, requests, 0)
    return (guided, state_norm[None, :], max_logit[None, :])


def solution(mesh):
    placed = (
        P("cfg", None, "seq", "tp"),
        P(None, None, "tp"),
        P(None, "tp"),
        P("tp", None),
        P("tp", None),
        P(),
        P(),
        P(),
        P("cfg", None),
        P(None, None, "seq"),
    )

    return jax.shard_map(
        local,
        mesh=mesh,
        in_specs=placed,
        out_specs=(P("cfg", "seq", "tp"), P("cfg", None), P("cfg", None)),
        check_vma=False,
    )
```

```python
import functools

import jax
import jax.numpy as jnp
from jax import lax
from jax.experimental import pallas as pl
from jax.experimental.pallas import tpu as pltpu
from jax.sharding import PartitionSpec as P


D = 3072
TXT = 512
SEQ_LEN = 1536
GRID = 32
HD = 128

norm_eps = 1e-06
rope_theta = 10000.0
guidance_scale = 4.0
rescale_share = 0.7
masked_value = -1e30

CHUNKS = 2


f32 = jnp.float32
bf16 = jnp.bfloat16

SWAP = [(i, i ^ 1) for i in range(8)]
CFG_SWAP = [(0, 1), (1, 0)]


def shift4(k):
    return [(i, ((i // 2 + k) % 4) * 2 + i % 2) for i in range(8)]


def owned_shard(g, z, i):
    return ((z + g) & 1) + 2 * (i ^ g)


def home_perm(i):
    return [
        (g * 8 + s, (s // 4) * 8 + owned_shard(g, s // 2, i) * 2 + s % 2)
        for g in range(2)
        for s in range(8)
    ]


def send(value, axes, pairs):
    return lax.ppermute(value, axes, pairs)


def together(*values):
    return lax.optimization_barrier(values)


def pick(array, index):
    return lax.dynamic_index_in_dim(array, index, 0, False)


VMEM = pl.BlockSpec(memory_space=pltpu.VMEM)
SMEM = pl.BlockSpec(memory_space=pltpu.SMEM)


HBM = pl.BlockSpec(memory_space=pltpu.HBM)


def call(kernel, outs, args, flops, specs, out_specs, scratch, grant):
    shapes = [jax.ShapeDtypeStruct(shape, dtype) for shape, dtype in outs]
    return pl.pallas_call(
        kernel,
        in_specs=specs,
        out_specs=out_specs,
        out_shape=shapes,
        scratch_shapes=scratch,
        compiler_params=pltpu.CompilerParams(vmem_limit_bytes=grant << 20),
        cost_estimate=pl.CostEstimate(
            flops=flops, transcendentals=0, bytes_accessed=sum(v.size * v.dtype.itemsize for v in args)
        ),
    )(*args)


def rotary(values, gain_row, cosine, sine, even):
    u = values * lax.rsqrt(jnp.mean(values * values, axis=-1, keepdims=True) + norm_eps) * gain_row
    turned = jnp.where(even, -pltpu.roll(u, HD - 1, 1), pltpu.roll(u, 1, 1))
    return u * cosine + turned * sine


def even_lanes(shape):
    return lax.broadcasted_iota(jnp.int32, shape, 1) % 2 == 0


LN_ROWS = 64
DOT_COLS = 256


def kv_kernel(order, *refs):
    blocks = refs[:8]
    scale_ref, shift_ref, w_ref, gain_ref, cos_ref, sin_ref, m_ref, kv_ref = refs[8:]
    rows, width = blocks[0].shape
    pieces = width // 128

    def norm(i, _):
        r = pl.ds(pl.multiple_of(i * LN_ROWS, LN_ROWS), LN_ROWS)

        def pieces_of(ref):
            return [ref[r, n * 128 : (n + 1) * 128].astype(f32) for n in range(pieces)]

        total = jnp.zeros((LN_ROWS, 128), f32)
        for ref in blocks:
            for v in pieces_of(ref):
                total = total + v
        mean = jnp.sum(total, axis=-1, keepdims=True) * (1.0 / D)
        square = jnp.zeros((LN_ROWS, 128), f32)
        for ref in blocks:
            for v in pieces_of(ref):
                center = v - mean
                square = square + center * center
        inverse = lax.rsqrt(jnp.sum(square, axis=-1, keepdims=True) * (1.0 / D) + norm_eps)
        for b, ref in enumerate(blocks):
            for n, v in enumerate(pieces_of(ref)):
                cols = pl.ds(pl.multiple_of(order[b] * width + n * 128, 128), 128)
                normed = (v - mean) * inverse
                m_ref[r, cols] = (scale_ref[:, cols] * normed + shift_ref[:, cols]).astype(bf16)
        return 0

    lax.fori_loop(0, rows // LN_ROWS, norm, 0, unroll=2)
    even = even_lanes((rows, HD))
    inner = w_ref.shape[1] // 2
    for n in range(w_ref.shape[1] // DOT_COLS):
        both = jnp.dot(
            m_ref[...], w_ref[:, n * DOT_COLS : (n + 1) * DOT_COLS], preferred_element_type=f32
        )
        for h in range(DOT_COLS // HD):
            v = both[:, h * HD : (h + 1) * HD]
            at = n * DOT_COLS + h * HD
            if at < inner:
                v = rotary(v, gain_ref[...], cos_ref[...], sin_ref[...], even)
            kv_ref[:, at : at + HD] = v.astype(bf16)


def keys_values(order, blocks, scale, shift, weight, gain, cosine, sine):
    rows = blocks[0].shape[0]
    args = (order, *blocks, scale, shift, weight, gain, cosine, sine)
    return call(
        kv_kernel,
        [((rows, D), bf16), ((rows, weight.shape[1]), bf16)],
        args,
        2 * rows * D * weight.shape[1],
        [SMEM] + [VMEM] * 14,
        [VMEM, VMEM],
        [],
        8,
    )


def qu_kernel(m_ref, wq_ref, wm_ref, wo_ref, gain_ref, cos_ref, sin_ref, q_ref, part_ref, u_ref):
    rows = m_ref.shape[0]
    even = even_lanes((rows, HD))
    for h in range(q_ref.shape[1] // HD):
        c = slice(h * HD, (h + 1) * HD)
        if h % 2 == 0:
            wide = slice(h * HD, min((h + 2) * HD, q_ref.shape[1]))
            pair = jnp.dot(m_ref[...], wq_ref[:, wide], preferred_element_type=f32)
        q = pair[:, (h % 2) * HD : (h % 2 + 1) * HD]
        q_ref[:, c] = rotary(q, gain_ref[...], cos_ref[...], sin_ref[...], even).astype(bf16)

    for n in range(wm_ref.shape[1] // DOT_COLS):
        c = slice(n * DOT_COLS, (n + 1) * DOT_COLS)
        u = jnp.dot(m_ref[...], wm_ref[:, c], preferred_element_type=f32)
        u_ref[:, c] = jax.nn.gelu(u, approximate=True).astype(bf16)

    def part(n, _):
        c = pl.ds(pl.multiple_of(n * DOT_COLS, DOT_COLS), DOT_COLS)
        part_ref[:, c] = jnp.dot(u_ref[...], wo_ref[:, c], preferred_element_type=f32)
        return 0

    lax.fori_loop(0, D // DOT_COLS, part, 0, unroll=4)


def queries_units(modded, wq, wm, wo, gain, cosine, sine):
    rows = modded.shape[0]
    inner, hidden = wq.shape[1], wm.shape[1]
    args = (modded, wq, wm, wo, gain, cosine, sine)
    return call(
        qu_kernel,
        [((rows, inner), bf16), ((rows, D), f32)],
        args,
        2 * rows * D * (inner + 2 * hidden),
        [VMEM] * 7,
        [VMEM] * 2,
        [pltpu.VMEM((rows, hidden), bf16)],
        8,
    )


Q_ROWS = 192
LOG2E = 1.4426950408889634


def attention_kernel(order, place, q_ref, *refs):
    kvs = refs[:4]
    w_ref, part_ref, far_ref, near_ref, peak_ref, o_ref = refs[4:]
    rows, inner = o_ref.shape
    width = far_ref.shape[2]
    piece = rows // 4
    z, y, length = place[0], place[1], place[2]
    lane = lax.broadcasted_iota(jnp.int32, (1, rows), 1)
    block = sum((lane >= k * piece).astype(jnp.int32) for k in range(1, 4))
    biases = []
    for n in range(4):
        shard = 2 * ((z - block) & 3) + (y if n < 2 else 1 - y)
        position = shard * (2 * piece) + (n % 2) * piece + lane - block * piece
        usable = (position >= TXT) | (position < length)
        biases.append(jnp.where(usable, 0.0, masked_value).astype(f32))
    contract = (((1,), (1,)), ((), ()))
    scale = HD ** (-0.5)

    def tile(i, top):
        r = pl.ds(pl.multiple_of(i * Q_ROWS, Q_ROWS), Q_ROWS)
        for h in range(inner // HD):
            c = slice(h * HD, (h + 1) * HD)
            cv = slice(inner + h * HD, inner + (h + 1) * HD)
            q = q_ref[r, c]
            logits = [
                lax.dot_general(q, kv[:, c], contract, preferred_element_type=f32) + bias
                for kv, bias in zip(kvs, biases)
            ]
            peak = functools.reduce(jnp.maximum, [jnp.max(s, axis=-1, keepdims=True) for s in logits])
            total, mix = None, None
            for kv, s in zip(kvs, logits):
                w = jnp.exp2((s - peak) * (scale * LOG2E))
                part = jnp.sum(w, axis=-1, keepdims=True)
                prod = jnp.dot(w.astype(bf16), kv[:, cv], preferred_element_type=f32)
                total = part if total is None else total + part
                mix = prod if mix is None else mix + prod
            o_ref[r, c] = (mix / total).astype(bf16)
            top = jnp.maximum(top, jnp.max(peak))
        return top

    top = lax.fori_loop(0, rows // Q_ROWS, tile, f32(masked_value))
    peak_ref[...] = jnp.full(peak_ref.shape, top * scale, f32)
    for n in range(8):
        cols = pl.ds(pl.multiple_of(order[n] * width, 128), width)
        out = part_ref[:, cols] + jnp.dot(o_ref[...], w_ref[:, cols], preferred_element_type=f32)
        if n < 4:
            far_ref[n] = out.astype(bf16)
        else:
            near_ref[n - 4] = out


def attention(order, place, q, kvs, w_attn_out, parts):
    rows, inner = q.shape
    args = (order, place, q, *kvs, w_attn_out, parts)
    return call(
        attention_kernel,
        [((4, rows, D // 8), bf16), ((4, rows, D // 8), f32), ((8, 128), f32)],
        args,
        24 * rows * rows * inner,
        [SMEM] * 2 + [VMEM] * 7,
        [VMEM] * 3,
        [pltpu.VMEM((rows, inner), bf16)],
        8,
    )


def join_kernel(near_ref, got_ref, *out_refs):
    for n, o_ref in enumerate(out_refs):
        o_ref[...] = (near_ref[n] + got_ref[n].astype(f32)).astype(o_ref.dtype)


def join_cores(near, got):
    _, rows, width = near.shape
    return call(
        join_kernel,
        [((rows, width), f32)] + [((rows, width), bf16)] * 3,
        (near, got),
        near.size,
        [VMEM] * 2,
        [VMEM] * 4,
        [],
        8,
    )


def rotary_tables(pos_ids, z, y, w_qkv):
    local_len = pos_ids.shape[2]
    image = (2 * z + y) * local_len + jnp.arange(local_len, dtype=jnp.int32) - TXT
    is_image = (image >= 0)[None, :]
    row_offset = jnp.max(jnp.where(is_image, pos_ids[:, 1] - (image // GRID)[None, :], -1), axis=1)
    col_offset = jnp.max(jnp.where(is_image, pos_ids[:, 2] - (image % GRID)[None, :], -1), axis=1)
    mine = jnp.stack([row_offset, col_offset], axis=0)
    above = send(mine, "seq", shift4(3))
    above, w_qkv = together(above, w_qkv)
    offsets = jnp.where(z == 0, above, mine)
    offsets = lax.dynamic_index_in_dim(offsets, z, 1, False)
    blocks = jnp.arange(4, dtype=jnp.int32)
    shard = 2 * ((z - blocks) & 3) + y
    part = local_len // CHUNKS
    start = jnp.arange(CHUNKS, dtype=jnp.int32)[:, None, None] * part + jnp.arange(part, dtype=jnp.int32)
    position = (shard[None, :, None] * local_len + start).reshape(-1)
    index = position - TXT
    pair_index = jnp.arange(HD, dtype=jnp.int32) // 2
    first_end = HD // 16
    second = first_end + (HD - HD // 8) // 4
    axis_of = jnp.where(pair_index < first_end, 0, jnp.where(pair_index < second, 1, 2))
    start = jnp.where(axis_of == 0, 0, jnp.where(axis_of == 1, first_end, second))
    span = jnp.where(axis_of == 0, HD // 8, (HD - HD // 8) // 2)
    frequency = jnp.power(f32(rope_theta), -2.0 * (pair_index - start).astype(f32) / span.astype(f32))
    row_id = jnp.where(index >= 0, index // GRID + offsets[0], 0).astype(f32)
    col_id = jnp.where(index >= 0, index % GRID + offsets[1], 0).astype(f32)
    angles = row_id[:, None] * jnp.where(axis_of == 1, frequency, 0.0)[None, :]
    angles = angles + col_id[:, None] * jnp.where(axis_of == 2, frequency, 0.0)[None, :]
    return jnp.cos(angles), jnp.sin(angles), w_qkv, above


def reduce_all(vector, sums):
    lane = lax.broadcasted_iota(jnp.int32, vector.shape, 1)
    every = jnp.broadcast_to(vector[None], (128,) + vector.shape)
    every = lax.all_to_all(every, ("cfg", "seq", "tp"), 0, 0, tiled=True)
    return jnp.where(lane < sums, jnp.sum(every, axis=0), jnp.max(every, axis=0))


def local(
    hidden_in, w_qkv, w_mlp, w_attn_out, w_mlp_out, mod_table, qk_gain, timestep, text_len, pos_ids
):
    tokens = hidden_in[0]
    requests, local_len, width = tokens.shape
    inner = w_qkv.shape[2]
    group = lax.axis_index("cfg")
    seq = lax.axis_index("seq")
    z, y = seq >> 1, seq & 1
    tp = lax.axis_index("tp")
    x, core = tp >> 1, tp & 1

    part = local_len // CHUNKS
    rows = 4 * part
    steps = jnp.arange(4, dtype=jnp.int32)
    back = 2 * ((x - steps) & 3)
    order = jnp.concatenate([back + core, back + 1 - core]).astype(jnp.int32)
    ahead = 2 * ((x + steps) & 3)
    out_order = jnp.concatenate([ahead + 1 - core, ahead + core]).astype(jnp.int32)

    moved = [pick(tokens, z)] + [
        send(pick(tokens, (z + k) & 3), "seq", shift4(k)) for k in range(1, 4)
    ]
    owns = [
        jnp.concatenate([block[n * part : (n + 1) * part] for block in moved], axis=0)
        for n in range(CHUNKS)
    ]
    from_x = [[own] + [send(own, "tp", shift4(k)) for k in range(1, 4)] for own in owns]
    owns_later, pos_ids, mod_table = together(owns, pos_ids, mod_table)

    mine = [(z - owned_shard(group, z, i)) & 3 for i in range(2)]
    theirs = [(z - owned_shard(1 - group, z, i)) & 3 for i in range(2)]

    def some(array, which):
        return jnp.stack([pick(array.reshape(4, part, width), k) for k in which], axis=0)

    modulation = pick(mod_table, pick(timestep, z))
    scale, shift = 1.0 + modulation[1:2], modulation[0:1]
    cosine, sine, w_qkv, above = rotary_tables(pos_ids, z, y, w_qkv)
    span = lambda v, n: v[n * rows : (n + 1) * rows]
    length = pick(text_len[0], z)

    gain_q, gain_k = qk_gain[0:1], qk_gain[1:2]
    wkv = w_qkv[:, 1:].reshape(D, 2 * inner)
    half = requests // 2
    theirs_in = jnp.stack([some(own, theirs) for own in owns_later])
    tokens, above = together(tokens, above)
    other_in = lax.dynamic_slice_in_dim(tokens, half * (1 - group), half, 0)
    place = jnp.stack([z, y, length]).astype(jnp.int32)
    cosines = [span(cosine, n) for n in range(CHUNKS)]
    sines = [span(sine, n) for n in range(CHUNKS)]
    (from_x[0], wkv, theirs_in, other_in, place, cosines, sines, order, out_order, scale, shift) = together(
        from_x[0], wkv, theirs_in, other_in, place, cosines, sines, order, out_order, scale, shift
    )
    modded, kvs = [], []
    for n in range(CHUNKS):
        blocks = from_x[n]
        if n:
            blocks, kvs[n - 1] = together(blocks, kvs[n - 1])
        blocks = blocks + [send(block, "tp", SWAP) for block in blocks]
        m, kv = keys_values(
            order, blocks, scale, shift, wkv, gain_k, cosines[n], sines[n]
        )
        modded.append(m)
        kvs.append(kv)
    w_qkv, kvs[-1] = together(w_qkv, kvs[-1])
    wq = w_qkv[:, 0]
    fars = [send(kvs[n], "seq", SWAP) for n in range(CHUNKS)]
    early = [
        queries_units(modded[n], wq, w_mlp, w_mlp_out, gain_q, cosines[n], sines[n])
        for n in range(CHUNKS)
    ]
    early, fars[-1] = together(early, fars[-1])
    kvs = kvs + fars

    peaks, joins = [], []
    for n in range(CHUNKS):
        queries, parts = early[n]
        if n:
            queries, joins[n - 1] = together(queries, joins[n - 1])
        far_part, near_part, peak = attention(out_order, place, queries, kvs, w_attn_out, parts)
        peaks.append(peak[0:1])
        got = send(far_part, "tp", SWAP)
        joins.append(join_cores(near_part, got))
    hidden_far = send(theirs_in, "cfg", CFG_SWAP)
    other = send(other_in, "cfg", CFG_SWAP)
    landings = [[send(joins[n][k], "tp", shift4(k)) for k in range(1, 4)] for n in range(CHUNKS)]
    for n in range(CHUNKS - 1):
        landings[n], joins[n + 1] = together(landings[n], joins[n + 1])

    joins[-1], mod_table, owns, tokens = together(joins[-1], mod_table, owns, tokens)
    kept = lax.dynamic_slice_in_dim(tokens, half * group, half, 0)
    gate = lax.dynamic_slice(mod_table, (pick(timestep, z), 2, tp * width), (1, 1, width))[0]
    own_square, raw_square, changes = f32(0), f32(0), []
    outgoing = change = None

    for n in range(CHUNKS):
        if n:
            outgoing, landings[n], joins[n] = together(outgoing, landings[n], joins[n])
        branch = joins[n][0]
        for arrived in landings[n]:
            branch = branch + arrived.astype(f32)
        delta = gate * branch
        state = owns[n].astype(f32) + delta
        own_square = own_square + jnp.sum(state * state)
        outgoing = some(delta.astype(bf16), theirs)
        delta_far = send(outgoing, "cfg", CFG_SWAP)
        if n == 0:
            delta_far, hidden_far = together(delta_far, hidden_far)
        delta_far = delta_far.astype(f32)
        delta_near = some(delta, mine)
        near = some(owns[n], mine).astype(f32) + delta_near
        hidden = hidden_far[n]
        if n:
            hidden, change = together(hidden, change)
            changes.append(change)
        far = hidden.astype(f32) + delta_far
        conditional = jnp.where(group == 0, near, far)
        unconditional = jnp.where(group == 0, far, near)
        raw = unconditional + guidance_scale * (conditional - unconditional)
        raw_square = raw_square + jnp.sum(raw * raw)
        cond_delta = jnp.where(group == 0, delta_near, delta_far)
        free_delta = jnp.where(group == 0, delta_far, delta_near)
        change = (free_delta + guidance_scale * (cond_delta - free_delta)).astype(bf16)
    changes.append(change)
    landed = [
        send(jnp.stack([c[i] for c in changes]), ("cfg", "seq"), home_perm(i)) for i in range(2)
    ]
    lane = lax.broadcasted_iota(jnp.int32, (1, 128), 1)
    here = group * requests + z
    vector = jnp.where(lane < 12, 0.0, masked_value)
    vector = jnp.where(lane == here, own_square, vector)
    vector = jnp.where(lane == 8 + z, raw_square, vector)
    vector = jnp.where(lane == 12 + here, functools.reduce(jnp.maximum, peaks), vector)
    vector = reduce_all(vector, 12)[0]
    vector, landed, other = together(vector, landed, other)

    flip = (z & 1) ^ (z >> 1) == 1
    change = jnp.stack([jnp.where(flip, landed[1 - i], landed[i]) for i in range(2)], axis=0)
    change = change.reshape(half, local_len, width).astype(f32)
    entries = float(SEQ_LEN * D)
    norm = jnp.sqrt(vector[:12] / entries + norm_eps)
    factors = rescale_share * norm[:4] / norm[8:] + (1.0 - rescale_share)
    factor = lax.dynamic_slice_in_dim(factors, half * group, half, 0)
    cond_in = jnp.where(group == 0, kept, other).astype(f32)
    free_in = jnp.where(group == 0, other, kept).astype(f32)
    base = free_in + guidance_scale * (cond_in - free_in)
    raw = base + change
    guided = (raw * factor[:, None, None]).astype(bf16)
    state_norm = lax.dynamic_slice_in_dim(norm, group * requests, requests, 0)
    max_logit = lax.dynamic_slice_in_dim(vector, 12 + group * requests, requests, 0)
    return (guided, state_norm[None, :], max_logit[None, :])


def solution(mesh):
    placed = (
        P("cfg", None, "seq", "tp"),
        P(None, None, "tp"),
        P(None, "tp"),
        P("tp", None),
        P("tp", None),
        P(),
        P(),
        P(),
        P("cfg", None),
        P(None, None, "seq"),
    )

    return jax.shard_map(
        local,
        mesh=mesh,
        in_specs=placed,
        out_specs=(P("cfg", "seq", "tp"), P("cfg", None), P("cfg", None)),
        check_vma=False,
    )
```
